128 devices in a mesh: gz: 32 (over x, z, y_lo), gx: 4 (over y_hi, core).
Axes of the slice: x: 4, y: 4 (y_hi: 2, y_lo: 2; y = y_hi * 2 + y_lo), z: 4, core: 2. Of those that a mesh axis runs over, the one named last changes fastest.
Arguments:
- velocity: float32 [256, 512, 512], P('gz', 'gx'), may hold values from -8 to 8
Outputs:
- detail_one: float32 [7, 128, 256, 256], P(None, 'gz', 'gx')
- detail_two: float32 [7, 64, 128, 128], P(None, 'gz', 'gx')
- detail_three: float32 [7, 32, 64, 64], P(None, 'gz', 'gx')
- coarse: float32 [32, 64, 64], P('gz', 'gx')
The draws below stay inside these ranges and needn't reach their ends.
All inputs are finite; a program needn't handle non-finite values.
Results may differ from the reference program's by a relative error of at most 0.00002.
Values sent between devices are 32-bit elements; how exact they have to be, the bound alone decides.
A program may use at most 64 MiB of HBM per device.

```python
import jax
import jax.numpy as jnp
from jax import lax

NX = 512
NY = 512
LEVELS = 3
NZ = 256


def block_scale(key, dims, pieces, low, top_value):
    level = 1.0
    for position, blocks in pieces:
        heights = jax.random.uniform(jax.random.fold_in(jax.random.fold_in(key, 6), position), (blocks,), jnp.float32, low / len(pieces), top_value / len(pieces))
        level = level * jnp.repeat(jnp.exp(heights), dims[position] // blocks).reshape((-1,) + (1,) * (len(dims) - 1 - position))
    return level


def scatter_about(rng, extent, deviation, limit, cuts=(), held_as=jnp.bfloat16):
    result = jax.random.normal(rng, extent, jnp.float32) * deviation
    if len(cuts) > 0:
        result = block_scale(rng, extent, cuts, -0.22, 0.18) * result
    return jnp.clip(result, min=-limit, max=limit).astype(held_as)


def setup_inputs(seed: int = 0) -> dict:
    seeds = jax.random.split(jax.random.key(seed), 2)
    return {
        "velocity": scatter_about(seeds[0], (NZ, NX, NY), 1.0, 8.0, ((0, 32), (1, 4)), jnp.float32),
    }


LOW_TAPS = (0.026748757411, -0.016864118443, -0.078223266529, 0.266864118443, 0.602949018236, 0.266864118443, -0.078223266529, -0.016864118443, 0.026748757411)
HIGH_TAPS = (0.091271763114, -0.057543526229, -0.591271763114, 1.115087052457, -0.591271763114, -0.057543526229, 0.091271763114)


def wrap_extend(field, along):
    count = field.shape[along]
    return jnp.concatenate([lax.slice_in_dim(field, count - 4, count, axis=along), field, lax.slice_in_dim(field, 0, 3, axis=along)], along)


def split_bands(extended, along, length):
    widths = [(0, 0)] * extended.ndim
    widths[along] = (0, 1)
    padded = jnp.pad(extended, widths)
    half = length // 2
    shape = padded.shape[:along] + (half + 4, 2) + padded.shape[along + 1:]
    phases = padded.reshape(shape)
    even_part = lax.index_in_dim(phases, 0, along + 1, keepdims=False)
    odd_part = lax.index_in_dim(phases, 1, along + 1, keepdims=False)
    low_band = jnp.zeros_like(lax.slice_in_dim(even_part, 0, half, axis=along))
    high_band = jnp.zeros_like(low_band)
    for offset in range(9):
        source = even_part if offset % 2 == 0 else odd_part
        start = offset // 2
        taken = lax.slice_in_dim(source, start, start + half, axis=along)
        low_band = low_band + LOW_TAPS[offset] * taken
        if offset >= 2:
            high_band = high_band + HIGH_TAPS[offset - 2] * taken
    return jnp.stack([low_band, high_band], 0)


def one_level(field):
    zbands = split_bands(wrap_extend(field, 0), 0, field.shape[0])
    xbands = split_bands(wrap_extend(zbands, 2), 2, field.shape[1])
    ybands = split_bands(wrap_extend(xbands, 4), 4, field.shape[2])
    return ybands.reshape((8,) + ybands.shape[3:])


def reference(velocity):
    approx = velocity.astype(jnp.float32)
    details = []
    for level_number in range(LEVELS):
        bands = one_level(approx)
        details.append(bands[1:])
        approx = bands[0]
    return details[0], details[1], details[2], approx
```

```python
import functools

import jax
import jax.numpy as jnp
import numpy as np
from jax import lax
from jax.experimental import pallas as pl
from jax.experimental.pallas import tpu as pltpu
from jax.sharding import PartitionSpec as P

LOW_TAPS = (
    0.026748757411,
    -0.016864118443,
    -0.078223266529,
    0.266864118443,
    0.602949018236,
    0.266864118443,
    -0.078223266529,
    -0.016864118443,
    0.026748757411,
)
HIGH_TAPS = (
    0.091271763114,
    -0.057543526229,
    -0.591271763114,
    1.115087052457,
    -0.591271763114,
    -0.057543526229,
    0.091271763114,
)

AL = -1.586134342059924
BE = -0.052980118572961
GA = 0.882911075530934
DE = 0.443506852043971
KL = 1.0 / 1.230174104914001
KH = 1.230174104914001
SCALE = (KL, KH)

MESH = pl.DeviceIdType.MESH
HIGHEST = lax.Precision.HIGHEST


def band_matrix(n):
    half = n // 2
    w = np.zeros((n, n), np.float64)
    for j in range(half):
        for k in range(9):
            w[(2 * j + k - 4) % n, j] += LOW_TAPS[k]
        for k in range(7):
            w[(2 * j + 1 + k - 3) % n, half + j] += HIGH_TAPS[k]
    return w.astype(np.float32)


def edge_terms(get, n):
    a = get(n - 1) + AL * get(n - 2)
    b = get(n - 2) + BE * (get(n - 3) + AL * (get(n - 4) + get(n - 2)) + a)
    e = get(0)
    c = e + BE * (get(1) + AL * (e + get(2)))
    return a, b, e, c


def lift_planes(f, a, b, e_up, c):
    even, odd = f[0::2], f[1::2]
    n = len(even)
    even_next = even[1:] + [e_up]
    d1 = [odd[j] + AL * (even[j] + even_next[j]) for j in range(n)]
    d1m = a + AL * even[0]
    d1_prev = [d1m] + d1[:-1]
    s1 = [even[j] + BE * (d1_prev[j] + d1[j]) for j in range(n)]
    s1m = b + (AL * BE) * even[0]
    s1n = c + BE * d1[-1]
    s1_next = s1[1:] + [s1n]
    d2 = [d1[j] + GA * (s1[j] + s1_next[j]) for j in range(n)]
    d2m = d1m + GA * (s1m + s1[0])
    d2_prev = [d2m] + d2[:-1]
    s2 = [s1[j] + DE * (d2_prev[j] + d2[j]) for j in range(n)]
    return s2, d2


def from_above(x, row):
    n = x.shape[0]
    at = lax.broadcasted_iota(jnp.int32, x.shape, 0)
    return jnp.where(at == n - 1, row, pltpu.roll(x, n - 1, 0))


def from_below(x, row):
    at = lax.broadcasted_iota(jnp.int32, x.shape, 0)
    return jnp.where(at == 0, row, pltpu.roll(x, 1, 0))


def lift_rows(even, odd, a, b, e_up, c):
    n = even.shape[0]
    d1 = odd + AL * (even + from_above(even, e_up))
    d1m = a + AL * even[0:1]
    s1 = even + BE * (from_below(d1, d1m) + d1)
    s1m = b + (AL * BE) * even[0:1]
    s1n = c + BE * d1[n - 1 : n]
    d2 = d1 + GA * (s1 + from_above(s1, s1n))
    d2m = d1m + GA * (s1m + s1[0:1])
    s2 = s1 + DE * (from_below(d2, d2m) + d2)
    return s2, d2


def dot(x, w):
    return jnp.dot(x, w, precision=HIGHEST, preferred_element_type=jnp.float32)


def kernel(
    nz, nx,
    v_hbm, w1_hbm, w2_hbm, w3_hbm,
    one_hbm, two_hbm, three_hbm, coarse_hbm,
    f1, w1, w2, w3, y1, xs1, xr1, own1, zs1, zr1,
    f2, y2, xs2, xr2, own2, zs2, zr2,
    f3, y3, xs3, xr3, own3, zs3, zr3, zr3b,
    one, two, three, coarse,
    in_sem, out_sem, xsend, xrecv, zsend, zrecv,
):
    iz, ix = lax.axis_index("gz"), lax.axis_index("gx")
    right, left = lax.rem(ix + 1, nx), lax.rem(ix + nx - 1, nx)
    up, down = lax.rem(iz + 1, nz), lax.rem(iz + nz - 1, nz)
    up2, down2 = lax.rem(iz + 2, nz), lax.rem(iz + nz - 2, nz)

    barrier = pltpu.get_barrier_semaphore()
    for k in (right, left):
        pl.semaphore_signal(barrier, inc=1, device_id={"gx": k}, device_id_type=MESH)
    for k in (up, down, up2, down2):
        pl.semaphore_signal(barrier, inc=1, device_id={"gz": k}, device_id_type=MESH)

    loads = [
        pltpu.make_async_copy(src, dst, in_sem.at[i])
        for i, (src, dst) in enumerate(
            [(v_hbm, f1), (w1_hbm, w1), (w2_hbm, w2), (w3_hbm, w3)]
        )
    ]
    for load in loads:
        load.start()

    sent = []

    def send(src, dst, send_sem, recv_sem, device):
        copy = pltpu.make_async_remote_copy(
            src_ref=src, dst_ref=dst, send_sem=send_sem, recv_sem=recv_sem,
            device_id=device, device_id_type=MESH,
        )
        copy.start()
        sent.append(copy)
        return copy

    def send_x(level, xs, xr):
        return [
            send(xs.at[0:2], xr.at[0:2], xsend.at[level, 0], xrecv.at[level, 0], {"gx": right}),
            send(xs.at[2:4], xr.at[2:4], xsend.at[level, 1], xrecv.at[level, 1], {"gx": left}),
        ]

    def send_z(slot, zs, zr, groups):
        return [
            send(zs.at[0, groups], zr.at[0, groups], zsend.at[slot, 0], zrecv.at[slot, 0], {"gz": up}),
            send(zs.at[1, groups], zr.at[1, groups], zsend.at[slot, 1], zrecv.at[slot, 1], {"gz": down}),
        ]

    stores = []

    def store(src, dst):
        copy = pltpu.make_async_copy(src, dst, out_sem.at[len(stores)])
        copy.start()
        stores.append(copy)

    def arrive(copies):
        for copy in copies:
            copy.wait_recv()

    def x_split(y, xr, own, columns):
        planes, half = y.shape[1], y.shape[2] // 2
        wide = max(1, y.shape[0] // 2)

        def plane(p):
            for column in columns:
                yb, at = column // wide, 128 * (column % wide)
                even = y[column, p, pl.ds(0, half, stride=2), :]
                odd = y[column, p, pl.ds(1, half, stride=2), :]
                terms = [xr[k, column, pl.ds(p, 1), :] for k in range(4)]
                low, high = lift_rows(even, odd, *terms)
                own[2 * yb, p, :, pl.ds(at, 128)] = low
                own[2 * yb + 1, p, :, pl.ds(at, 128)] = high

        if planes == 8:
            lax.fori_loop(0, planes, lambda p, _: (plane(p), 0)[1], 0)
        else:
            for p in range(planes):
                plane(p)

    def z_terms(own, zs, groups, step):
        planes, rows = own.shape[1], own.shape[2]
        for g in groups:
            def chunk(i, _):
                at = pl.ds(pl.multiple_of(i * step, step), step)
                terms = edge_terms(lambda k: own[g, k, at, :], planes)
                for k in range(4):
                    zs[k // 2, g, k % 2, at, :] = terms[k]
                return 0

            lax.fori_loop(0, rows // step, chunk, 0)

    def z_split(own, zr, g, step, low_to, high_to):
        planes, rows = own.shape[1], own.shape[2]

        def chunk(i, _):
            at = pl.ds(pl.multiple_of(i * step, step), step)
            f = [own[g, k, at, :] for k in range(planes)]
            terms = [zr[k // 2, g, k % 2, at, :] for k in range(4)]
            low, high = lift_planes(f, *terms)
            for j in range(planes // 2):
                low_to[j, at, :] = low[j] * (KL * SCALE[g % 2])
                high_to[j, at, :] = high[j] * (KH * SCALE[g % 2])
            return 0

        lax.fori_loop(0, rows // step, chunk, 0)

    def bands(out, g):
        return out.at[2 * g - 1], out.at[2 * g]

    loads[0].wait()
    loads[1].wait()
    edges = edge_terms(lambda k: f1[:, k, :], f1.shape[1])
    out = dot(jnp.concatenate(edges, 0), w1[...])
    for k in range(4):
        for c in range(4):
            xs1[k, c] = out[8 * k : 8 * k + 8, 128 * c : 128 * c + 128]
    pl.semaphore_wait(barrier, 6)
    x1 = send_x(0, xs1, xr1)
    planes = f1.shape[0]
    for yb in range(2):
        lanes = pl.ds(256 * yb, 256)

        def rows(i, _):
            at = pl.ds(2 * i, 2)
            out = dot(f1[at].reshape(256, 512), w1[:, lanes])
            for c in range(2):
                y1[2 * yb + c, at] = out[:, 128 * c : 128 * c + 128].reshape(2, 128, 128)
            return 0

        lax.fori_loop(0, planes // 2, rows, 0)
        if yb == 0:
            arrive(x1)
        x_split(y1, xr1, own1, (2 * yb, 2 * yb + 1))
        z_terms(own1, zs1, (2 * yb, 2 * yb + 1), 16)
        if yb == 0:
            z1 = [send_z(0, zs1, zr1, 0), send_z(1, zs1, zr1, 1)]
        else:
            z1 += [send_z(2, zs1, zr1, 2), send_z(3, zs1, zr1, 3)]

    arrive(z1[0])
    z_split(own1, zr1, 0, 8, f2, one.at[0])
    store(one.at[0:1], one_hbm.at[0:1])

    loads[2].wait()
    out = dot(f2[...].reshape(256, 256), w2[...])
    for c in range(2):
        y2[c] = out[:, 128 * c : 128 * c + 128].reshape(4, 64, 128)
        for k, term in enumerate(edge_terms(lambda k: y2[c, :, k, :], 64)):
            xs2[k, c] = term
    x2 = send_x(1, xs2, xr2)
    arrive(x2)
    x_split(y2, xr2, own2, (0, 1))
    z_terms(own2, zs2, range(4), 32)
    z2 = [send_z(4, zs2, zr2, 0), send_z(5, zs2, zr2, pl.ds(1, 3))]
    arrive(z2[0])
    z_split(own2, zr2, 0, 32, f3, two.at[0])
    store(two.at[0:1], two_hbm.at[0:1])

    loads[3].wait()
    y3[0] = dot(f3[...].reshape(64, 128), w3[...]).reshape(2, 32, 128)
    for k, term in enumerate(edge_terms(lambda k: y3[0, :, k, :], 32)):
        xs3[k, 0] = term
    x3 = send_x(2, xs3, xr3)
    arrive(x3)
    x_split(y3, xr3, own3, (0,))
    for xb in range(2):
        even, odd = own3[xb, 0], own3[xb, 1]
        a = odd + AL * even
        zs3[0, xb] = a
        zs3[1, xb] = even + BE * (AL * even + a)
        zs3[2, xb] = even
        zs3[3, xb] = even + BE * (odd + AL * even)
    z3 = [
        send(zs3.at[0:2], zr3.at[0:2], zsend.at[6, 0], zrecv.at[6, 0], {"gz": up}),
        send(zs3.at[2:4], zr3.at[2:4], zsend.at[6, 1], zrecv.at[6, 1], {"gz": down}),
        send(zs3.at[0:1], zr3b.at[0:1], zsend.at[7, 0], zrecv.at[7, 0], {"gz": up2}),
        send(zs3.at[2:3], zr3b.at[1:2], zsend.at[7, 1], zrecv.at[7, 1], {"gz": down2}),
    ]
    for g in (1, 2):
        arrive(z1[g])
        z_split(own1, zr1, g, 8, *bands(one, g))
        store(one.at[2 * g - 1 : 2 * g + 1], one_hbm.at[2 * g - 1 : 2 * g + 1])
    arrive(z3)
    for xb in range(2):
        a, b, e, c = (zr3[k, xb] for k in range(4))
        b = b + BE * zr3b[0, xb]
        c = c + (AL * BE) * zr3b[1, xb]
        low, high = lift_planes([own3[xb, 0], own3[xb, 1]], a, b, e, c)
        low, high = low[0] * (KL * SCALE[xb]), high[0] * (KH * SCALE[xb])
        for yb in range(2):
            lanes = slice(64 * yb, 64 * yb + 64)
            band = 2 * xb + 4 * yb
            if band == 0:
                coarse[0] = low[:, lanes]
            else:
                three[band - 1, 0] = low[:, lanes]
            three[band, 0] = high[:, lanes]
    store(coarse, coarse_hbm)
    store(three, three_hbm)
    arrive(z2[1])
    for g in (1, 2, 3):
        z_split(own2, zr2, g, 32, *bands(two, g))
    store(two.at[1:7], two_hbm.at[1:7])
    arrive(z1[3])
    z_split(own1, zr1, 3, 8, *bands(one, 3))
    store(one.at[5:7], one_hbm.at[5:7])
    for copy in sent:
        copy.wait_send()
    for copy in stores:
        copy.wait()


def on_device(nz, nx, velocity):
    f32 = jnp.float32
    shapes = [(7, 4, 64, 256), (7, 2, 32, 128), (7, 1, 16, 64), (1, 16, 64)]
    scratch = [
        (8, 128, 512), (512, 512), (256, 256), (128, 128),
        (4, 8, 128, 128), (4, 4, 8, 128), (4, 4, 8, 128), (4, 8, 64, 256), (2, 4, 2, 64, 256), (2, 4, 2, 64, 256),
        (4, 64, 256), (2, 4, 64, 128), (4, 2, 4, 128), (4, 2, 4, 128), (4, 4, 32, 128), (2, 4, 2, 32, 128), (2, 4, 2, 32, 128),
        (2, 32, 128), (1, 2, 32, 128), (4, 1, 2, 128), (4, 1, 2, 128), (2, 2, 16, 128), (4, 2, 16, 128), (4, 2, 16, 128), (2, 2, 16, 128),
    ] + shapes
    dma = pltpu.SemaphoreType.DMA
    hbm = pl.BlockSpec(memory_space=pl.ANY)
    return pl.pallas_call(
        functools.partial(kernel, nz, nx),
        out_shape=tuple(jax.ShapeDtypeStruct(s, f32) for s in shapes),
        in_specs=[hbm] * 4,
        out_specs=(hbm,) * 4,
        scratch_shapes=[pltpu.VMEM(s, f32) for s in scratch]
        + [dma((4,)), dma((8,)), dma((3, 2)), dma((3, 2)), dma((8, 2)), dma((8, 2))],
        compiler_params=pltpu.CompilerParams(collective_id=0, has_side_effects=True),
        name="wavelet",
    )(velocity, *(jnp.asarray(band_matrix(n)) for n in (512, 256, 128)))


def solution(mesh):
    return jax.shard_map(
        functools.partial(on_device, mesh.shape["gz"], mesh.shape["gx"]),
        mesh=mesh,
        in_specs=(P("gz", "gx", None),),
        out_specs=(
            P(None, "gz", "gx", None),
            P(None, "gz", "gx", None),
            P(None, "gz", "gx", None),
            P("gz", "gx", None),
        ),
        check_vma=False,
    )
```

```python
import functools

import jax
import jax.numpy as jnp
import numpy as np
from jax import lax
from jax.experimental import pallas as pl
from jax.experimental.pallas import tpu as pltpu
from jax.sharding import PartitionSpec as P

LOW_TAPS = (
    0.026748757411,
    -0.016864118443,
    -0.078223266529,
    0.266864118443,
    0.602949018236,
    0.266864118443,
    -0.078223266529,
    -0.016864118443,
    0.026748757411,
)
HIGH_TAPS = (
    0.091271763114,
    -0.057543526229,
    -0.591271763114,
    1.115087052457,
    -0.591271763114,
    -0.057543526229,
    0.091271763114,
)

AL = -1.586134342059924
BE = -0.052980118572961
GA = 0.882911075530934
DE = 0.443506852043971
KL = 1.0 / 1.230174104914001
KH = 1.230174104914001
SCALE = (KL, KH)

MESH = pl.DeviceIdType.MESH
HIGHEST = lax.Precision.HIGHEST


def band_matrix(n):
    half = n // 2
    w = np.zeros((n, n), np.float64)
    for j in range(half):
        for k in range(9):
            w[(2 * j + k - 4) % n, j] += LOW_TAPS[k]
        for k in range(7):
            w[(2 * j + 1 + k - 3) % n, half + j] += HIGH_TAPS[k]
    return w.astype(np.float32)


def edge_terms(get, n):
    a = get(n - 1) + AL * get(n - 2)
    b = get(n - 2) + BE * (get(n - 3) + AL * (get(n - 4) + get(n - 2)) + a)
    e = get(0)
    c = e + BE * (get(1) + AL * (e + get(2)))
    return a, b, e, c


def lift_planes(f, a, b, e_up, c):
    even, odd = f[0::2], f[1::2]
    n = len(even)
    even_next = even[1:] + [e_up]
    d1 = [odd[j] + AL * (even[j] + even_next[j]) for j in range(n)]
    d1m = a + AL * even[0]
    d1_prev = [d1m] + d1[:-1]
    s1 = [even[j] + BE * (d1_prev[j] + d1[j]) for j in range(n)]
    s1m = b + (AL * BE) * even[0]
    s1n = c + BE * d1[-1]
    s1_next = s1[1:] + [s1n]
    d2 = [d1[j] + GA * (s1[j] + s1_next[j]) for j in range(n)]
    d2m = d1m + GA * (s1m + s1[0])
    d2_prev = [d2m] + d2[:-1]
    s2 = [s1[j] + DE * (d2_prev[j] + d2[j]) for j in range(n)]
    return s2, d2


def from_above(x, row):
    n = x.shape[0]
    at = lax.broadcasted_iota(jnp.int32, x.shape, 0)
    return jnp.where(at == n - 1, row, pltpu.roll(x, n - 1, 0))


def from_below(x, row):
    at = lax.broadcasted_iota(jnp.int32, x.shape, 0)
    return jnp.where(at == 0, row, pltpu.roll(x, 1, 0))


def lift_rows(even, odd, a, b, e_up, c):
    n = even.shape[0]
    d1 = odd + AL * (even + from_above(even, e_up))
    d1m = a + AL * even[0:1]
    s1 = even + BE * (from_below(d1, d1m) + d1)
    s1m = b + (AL * BE) * even[0:1]
    s1n = c + BE * d1[n - 1 : n]
    d2 = d1 + GA * (s1 + from_above(s1, s1n))
    d2m = d1m + GA * (s1m + s1[0:1])
    s2 = s1 + DE * (from_below(d2, d2m) + d2)
    return s2, d2


def dot(x, w):
    return jnp.dot(x, w, precision=HIGHEST, preferred_element_type=jnp.float32)


def kernel(
    nz, nx,
    v_hbm, w1_hbm, w2_hbm, w3_hbm,
    one, two, three, coarse,
    f1, w1, w2, w3, y1, xs1, xr1, own1, zs1, zr1,
    f2, y2, xs2, xr2, own2, zs2, zr2,
    f3, y3, xs3, xr3, own3, zs3, zr3, zr3b,
    in_sem, xsend, xrecv, zsend, zrecv, usend, urecv,
):
    iz, ix = lax.axis_index("gz"), lax.axis_index("gx")
    right, left = lax.rem(ix + 1, nx), lax.rem(ix + nx - 1, nx)
    up, down = lax.rem(iz + 1, nz), lax.rem(iz + nz - 1, nz)
    up2, down2 = lax.rem(iz + 2, nz), lax.rem(iz + nz - 2, nz)

    barrier = pltpu.get_barrier_semaphore()
    for k in (right, left):
        pl.semaphore_signal(barrier, inc=1, device_id={"gx": k}, device_id_type=MESH)
    for k in (up, down, up2, down2):
        pl.semaphore_signal(barrier, inc=1, device_id={"gz": k}, device_id_type=MESH)

    loads = [
        pltpu.make_async_copy(src, dst, in_sem.at[i])
        for i, (src, dst) in enumerate(
            [(v_hbm, f1), (w1_hbm, w1), (w2_hbm, w2), (w3_hbm, w3)]
        )
    ]
    for load in loads:
        load.start()

    sent = []

    def send(src, dst, send_sem, recv_sem, device):
        copy = pltpu.make_async_remote_copy(
            src_ref=src, dst_ref=dst, send_sem=send_sem, recv_sem=recv_sem,
            device_id=device, device_id_type=MESH,
        )
        copy.start()
        sent.append(copy)
        return copy

    def send_x(level, xs, xr):
        return [
            send(xs.at[0:2], xr.at[0:2], xsend.at[level, 0], xrecv.at[level, 0], {"gx": right}),
            send(xs.at[2:4], xr.at[2:4], xsend.at[level, 1], xrecv.at[level, 1], {"gx": left}),
        ]

    def send_z(slot, zs, zr, groups):
        return [
            send(zs.at[0, groups], zr.at[0, groups], zsend.at[slot, 0], zrecv.at[slot, 0], {"gz": up}),
            send(zs.at[1, groups], zr.at[1, groups], zsend.at[slot, 1], zrecv.at[slot, 1], {"gz": down}),
        ]

    units = [(g, k, r) for g in (1, 2, 3) for k in range(2) for r in range(2)]
    pending = list(units)
    on_way = {1: [], 2: [], 3: []}

    def send_units(count):
        for _ in range(min(count, len(pending))):
            g, k, r = pending.pop(0)
            at = pl.ds(32 * r, 32)
            for d, device in ((0, {"gz": up}), (1, {"gz": down})):
                i = units.index((g, k, r))
                on_way[g].append(
                    send(zs1.at[d, g, k, at], zr1.at[d, g, k, at], usend.at[i, d], urecv.at[i, d], device)
                )

    def arrive(copies):
        for copy in copies:
            copy.wait_recv()

    def x_split(y, xr, own, columns):
        planes, half = y.shape[1], y.shape[2] // 2
        wide = max(1, y.shape[0] // 2)

        def plane(p):
            for column in columns:
                yb, at = column // wide, 128 * (column % wide)
                even = y[column, p, pl.ds(0, half, stride=2), :]
                odd = y[column, p, pl.ds(1, half, stride=2), :]
                terms = [xr[k, column, pl.ds(p, 1), :] for k in range(4)]
                low, high = lift_rows(even, odd, *terms)
                own[2 * yb, p, :, pl.ds(at, 128)] = low
                own[2 * yb + 1, p, :, pl.ds(at, 128)] = high

        if planes == 8:
            lax.fori_loop(0, planes, lambda p, _: (plane(p), 0)[1], 0)
        else:
            for p in range(planes):
                plane(p)

    def z_terms(own, zs, groups, step):
        planes, rows = own.shape[1], own.shape[2]
        for g in groups:
            def chunk(i, _):
                at = pl.ds(pl.multiple_of(i * step, step), step)
                terms = edge_terms(lambda k: own[g, k, at, :], planes)
                for k in range(4):
                    zs[k // 2, g, k % 2, at, :] = terms[k]
                return 0

            lax.fori_loop(0, rows // step, chunk, 0)

    def z_split(own, zr, g, step, low_to, high_to):
        planes, rows = own.shape[1], own.shape[2]

        def chunk(i, _):
            at = pl.ds(pl.multiple_of(i * step, step), step)
            f = [own[g, k, at, :] for k in range(planes)]
            terms = [zr[k // 2, g, k % 2, at, :] for k in range(4)]
            low, high = lift_planes(f, *terms)
            for j in range(planes // 2):
                low_to[j, at, :] = low[j] * (KL * SCALE[g % 2])
                high_to[j, at, :] = high[j] * (KH * SCALE[g % 2])
            return 0

        lax.fori_loop(0, rows // step, chunk, 0)

    def bands(out, g):
        return out.at[2 * g - 1], out.at[2 * g]

    loads[0].wait()
    loads[1].wait()
    edges = edge_terms(lambda k: f1[:, k, :], f1.shape[1])
    out = dot(jnp.concatenate(edges, 0), w1[...])
    for k in range(4):
        for c in range(4):
            xs1[k, c] = out[8 * k : 8 * k + 8, 128 * c : 128 * c + 128]
    pl.semaphore_wait(barrier, 6)
    x1 = send_x(0, xs1, xr1)
    planes = f1.shape[0]
    for yb in range(2):
        lanes = pl.ds(256 * yb, 256)

        def rows(i, _):
            at = pl.ds(2 * i, 2)
            out = dot(f1[at].reshape(256, 512), w1[:, lanes])
            for c in range(2):
                y1[2 * yb + c, at] = out[:, 128 * c : 128 * c + 128].reshape(2, 128, 128)
            return 0

        lax.fori_loop(0, planes // 2, rows, 0)
        if yb == 0:
            arrive(x1)
        x_split(y1, xr1, own1, (2 * yb, 2 * yb + 1))
        z_terms(own1, zs1, (2 * yb, 2 * yb + 1), 16)
        if yb == 0:
            z1 = send_z(0, zs1, zr1, 0)
            send_units(3)

    arrive(z1)
    z_split(own1, zr1, 0, 8, f2, one.at[0])

    loads[2].wait()
    out = dot(f2[...].reshape(256, 256), w2[...])
    for c in range(2):
        y2[c] = out[:, 128 * c : 128 * c + 128].reshape(4, 64, 128)
        for k, term in enumerate(edge_terms(lambda k: y2[c, :, k, :], 64)):
            xs2[k, c] = term
    x2 = send_x(1, xs2, xr2)
    send_units(2)
    arrive(x2)
    x_split(y2, xr2, own2, (0, 1))
    z_terms(own2, zs2, range(4), 32)
    z2 = send_z(1, zs2, zr2, 0)
    send_units(3)
    arrive(z2)
    z_split(own2, zr2, 0, 32, f3, two.at[0])

    loads[3].wait()
    y3[0] = dot(f3[...].reshape(64, 128), w3[...]).reshape(2, 32, 128)
    for k, term in enumerate(edge_terms(lambda k: y3[0, :, k, :], 32)):
        xs3[k, 0] = term
    x3 = send_x(2, xs3, xr3)
    send_units(2)
    arrive(x3)
    x_split(y3, xr3, own3, (0,))
    for xb in range(2):
        even, odd = own3[xb, 0], own3[xb, 1]
        a = odd + AL * even
        zs3[0, xb] = a
        zs3[1, xb] = even + BE * (AL * even + a)
        zs3[2, xb] = even
        zs3[3, xb] = even + BE * (odd + AL * even)
    z3 = [
        send(zs3.at[0:2], zr3.at[0:2], zsend.at[3, 0], zrecv.at[3, 0], {"gz": up}),
        send(zs3.at[2:4], zr3.at[2:4], zsend.at[3, 1], zrecv.at[3, 1], {"gz": down}),
        send(zs3.at[0:1], zr3b.at[0:1], zsend.at[4, 0], zrecv.at[4, 0], {"gz": up2}),
        send(zs3.at[2:3], zr3b.at[1:2], zsend.at[4, 1], zrecv.at[4, 1], {"gz": down2}),
    ]
    send_units(len(units))
    z2 = send_z(2, zs2, zr2, pl.ds(1, 3))
    for g in (1, 2):
        arrive(on_way[g])
        z_split(own1, zr1, g, 8, *bands(one, g))
    arrive(z3)
    for xb in range(2):
        a, b, e, c = (zr3[k, xb] for k in range(4))
        b = b + BE * zr3b[0, xb]
        c = c + (AL * BE) * zr3b[1, xb]
        low, high = lift_planes([own3[xb, 0], own3[xb, 1]], a, b, e, c)
        low, high = low[0] * (KL * SCALE[xb]), high[0] * (KH * SCALE[xb])
        for yb in range(2):
            lanes = slice(64 * yb, 64 * yb + 64)
            band = 2 * xb + 4 * yb
            if band == 0:
                coarse[0] = low[:, lanes]
            else:
                three[band - 1, 0] = low[:, lanes]
            three[band, 0] = high[:, lanes]
    arrive(on_way[3])
    z_split(own1, zr1, 3, 8, *bands(one, 3))
    arrive(z2)
    for g in (1, 2, 3):
        z_split(own2, zr2, g, 32, *bands(two, g))
    for copy in sent:
        copy.wait_send()


def place(one, two, three, coarse, one_to, two_to, three_to, coarse_to, sem):
    pairs = [(one.at[b], one_to.at[b]) for b in range(7)]
    pairs += [(two, two_to), (three, three_to), (coarse, coarse_to)]
    copies = [pltpu.make_async_copy(src, dst, sem.at[i]) for i, (src, dst) in enumerate(pairs)]
    for copy in copies:
        copy.start()
    for copy in copies:
        copy.wait()


def on_device(nz, nx, velocity):
    f32 = jnp.float32
    shapes = [(7, 4, 64, 256), (7, 2, 32, 128), (7, 1, 16, 64), (1, 16, 64)]
    scratch = [
        (8, 128, 512), (512, 512), (256, 256), (128, 128),
        (4, 8, 128, 128), (4, 4, 8, 128), (4, 4, 8, 128), (4, 8, 64, 256), (2, 4, 2, 64, 256), (2, 4, 2, 64, 256),
        (4, 64, 256), (2, 4, 64, 128), (4, 2, 4, 128), (4, 2, 4, 128), (4, 4, 32, 128), (2, 4, 2, 32, 128), (2, 4, 2, 32, 128),
        (2, 32, 128), (1, 2, 32, 128), (4, 1, 2, 128), (4, 1, 2, 128), (2, 2, 16, 128), (4, 2, 16, 128), (4, 2, 16, 128), (2, 2, 16, 128),
    ]
    dma = pltpu.SemaphoreType.DMA
    hbm = pl.BlockSpec(memory_space=pl.ANY)
    vmem = pl.BlockSpec(memory_space=pltpu.VMEM)
    results = pl.pallas_call(
        functools.partial(kernel, nz, nx),
        out_shape=tuple(pltpu.VMEM(s, f32) for s in shapes),
        in_specs=[hbm] * 4,
        out_specs=(vmem,) * 4,
        scratch_shapes=[pltpu.VMEM(s, f32) for s in scratch]
        + [dma((4,)), dma((3, 2)), dma((3, 2)), dma((5, 2)), dma((5, 2)), dma((12, 2)), dma((12, 2))],
        compiler_params=pltpu.CompilerParams(collective_id=0, has_side_effects=True),
        name="wavelet",
    )(velocity, *(jnp.asarray(band_matrix(n)) for n in (512, 256, 128)))
    return pl.pallas_call(
        place,
        out_shape=tuple(jax.ShapeDtypeStruct(s, f32) for s in shapes),
        in_specs=[vmem] * 4,
        out_specs=(hbm,) * 4,
        scratch_shapes=[dma((10,))],
        name="place",
    )(*(pltpu.with_memory_space_constraint(r, pltpu.VMEM) for r in results))


def solution(mesh):
    return jax.shard_map(
        functools.partial(on_device, mesh.shape["gz"], mesh.shape["gx"]),
        mesh=mesh,
        in_specs=(P("gz", "gx", None),),
        out_specs=(
            P(None, "gz", "gx", None),
            P(None, "gz", "gx", None),
            P(None, "gz", "gx", None),
            P("gz", "gx", None),
        ),
        check_vma=False,
    )
```

```python
import functools

import jax
import jax.numpy as jnp
import numpy as np
from jax import lax
from jax.experimental import pallas as pl
from jax.experimental.pallas import tpu as pltpu
from jax.sharding import PartitionSpec as P

LOW_TAPS = (
    0.026748757411,
    -0.016864118443,
    -0.078223266529,
    0.266864118443,
    0.602949018236,
    0.266864118443,
    -0.078223266529,
    -0.016864118443,
    0.026748757411,
)
HIGH_TAPS = (
    0.091271763114,
    -0.057543526229,
    -0.591271763114,
    1.115087052457,
    -0.591271763114,
    -0.057543526229,
    0.091271763114,
)

AL = -1.586134342059924
BE = -0.052980118572961
GA = 0.882911075530934
DE = 0.443506852043971
KL = 1.0 / 1.230174104914001
KH = 1.230174104914001
SCALE = (KL, KH)

MESH = pl.DeviceIdType.MESH
HIGHEST = lax.Precision.HIGHEST


def band_matrix(n):
    half = n // 2
    w = np.zeros((n, n), np.float64)
    for j in range(half):
        for k in range(9):
            w[(2 * j + k - 4) % n, j] += LOW_TAPS[k]
        for k in range(7):
            w[(2 * j + 1 + k - 3) % n, half + j] += HIGH_TAPS[k]
    return w.astype(np.float32)


def edge_terms(get, n):
    a = get(n - 1) + AL * get(n - 2)
    b = get(n - 2) + BE * (get(n - 3) + AL * (get(n - 4) + get(n - 2)) + a)
    e = get(0)
    c = e + BE * (get(1) + AL * (e + get(2)))
    return a, b, e, c


def lift_planes(f, a, b, e_up, c):
    even, odd = f[0::2], f[1::2]
    n = len(even)
    even_next = even[1:] + [e_up]
    d1 = [odd[j] + AL * (even[j] + even_next[j]) for j in range(n)]
    d1m = a + AL * even[0]
    d1_prev = [d1m] + d1[:-1]
    s1 = [even[j] + BE * (d1_prev[j] + d1[j]) for j in range(n)]
    s1m = b + (AL * BE) * even[0]
    s1n = c + BE * d1[-1]
    s1_next = s1[1:] + [s1n]
    d2 = [d1[j] + GA * (s1[j] + s1_next[j]) for j in range(n)]
    d2m = d1m + GA * (s1m + s1[0])
    d2_prev = [d2m] + d2[:-1]
    s2 = [s1[j] + DE * (d2_prev[j] + d2[j]) for j in range(n)]
    return s2, d2


def from_above(x, row):
    n = x.shape[0]
    at = lax.broadcasted_iota(jnp.int32, x.shape, 0)
    return jnp.where(at == n - 1, row, pltpu.roll(x, n - 1, 0))


def from_below(x, row):
    at = lax.broadcasted_iota(jnp.int32, x.shape, 0)
    return jnp.where(at == 0, row, pltpu.roll(x, 1, 0))


def lift_rows(even, odd, a, b, e_up, c):
    n = even.shape[0]
    d1 = odd + AL * (even + from_above(even, e_up))
    d1m = a + AL * even[0:1]
    s1 = even + BE * (from_below(d1, d1m) + d1)
    s1m = b + (AL * BE) * even[0:1]
    s1n = c + BE * d1[n - 1 : n]
    d2 = d1 + GA * (s1 + from_above(s1, s1n))
    d2m = d1m + GA * (s1m + s1[0:1])
    s2 = s1 + DE * (from_below(d2, d2m) + d2)
    return s2, d2


def deinterleave(n):
    p = np.zeros((n, n), np.float32)
    for j in range(n // 2):
        p[2 * j, j] = p[2 * j + 1, n // 2 + j] = 1.0
    return p


def lift_lanes(x, pick):
    even, odd = [], []
    for b in range(x.shape[1] // 256):
        block = x[:, 256 * b : 256 * b + 256]
        parts = []
        for _ in range(3):
            parts.append(block.astype(jnp.bfloat16))
            block = block - parts[-1].astype(jnp.float32)
        out = sum(jnp.dot(part, pick, preferred_element_type=jnp.float32) for part in parts)
        even.append(out[:, :128])
        odd.append(out[:, 128:])
    n = len(even)
    lane = lax.broadcasted_iota(jnp.int32, even[0].shape, 1)

    def following(v):
        moved = [pltpu.roll(u, 127, 1) for u in v]
        return moved if n == 1 else [jnp.where(lane == 127, moved[(i + 1) % n], moved[i]) for i in range(n)]

    def preceding(v):
        moved = [pltpu.roll(u, 1, 1) for u in v]
        return moved if n == 1 else [jnp.where(lane == 0, moved[(i - 1) % n], moved[i]) for i in range(n)]

    def step(v, factor, w, shifted):
        return [p + factor * (q + r) for p, q, r in zip(v, w, shifted(w))]

    d1 = step(odd, AL, even, following)
    s1 = step(even, BE, d1, preceding)
    d2 = step(d1, GA, s1, following)
    s2 = step(s1, DE, d2, preceding)
    return [KL * u for u in s2] + [KH * u for u in d2]


def halo_effect(a, b, e, c):
    first = (GA * BE) * a
    before = a + GA * (b + BE * a)
    q = AL * e
    last = q + GA * (c + (2 * BE) * q)
    last_but = (GA * BE) * q
    low = (BE * a + DE * (before + first), DE * first, DE * last_but, BE * q + DE * (last_but + last))
    return low, (first, last_but, last)


def dot(x, w):
    return jnp.dot(x, w, precision=HIGHEST, preferred_element_type=jnp.float32)


def kernel(
    nz, nx,
    v_hbm, pick_hbm, w3_hbm,
    one, two, three, coarse,
    f1, pick, w3, y1, yz1, xs1, xr1, own1, zs1, zr1,
    f2, y2, xs2, xr2, own2, zs2, zr2,
    f3, y3, xs3, xr3, own3, zs3, zr3, zr3b,
    in_sem, xsend, xrecv, zsend, zrecv, usend, urecv,
):
    iz, ix = lax.axis_index("gz"), lax.axis_index("gx")
    right, left = lax.rem(ix + 1, nx), lax.rem(ix + nx - 1, nx)
    up, down = lax.rem(iz + 1, nz), lax.rem(iz + nz - 1, nz)
    up2, down2 = lax.rem(iz + 2, nz), lax.rem(iz + nz - 2, nz)

    barrier = pltpu.get_barrier_semaphore()
    for k in (right, left):
        pl.semaphore_signal(barrier, inc=1, device_id={"gx": k}, device_id_type=MESH)
    for k in (up, down, up2, down2):
        pl.semaphore_signal(barrier, inc=1, device_id={"gz": k}, device_id_type=MESH)

    loads = [
        pltpu.make_async_copy(src, dst, in_sem.at[i])
        for i, (src, dst) in enumerate(
            [(v_hbm, f1), (pick_hbm, pick), (w3_hbm, w3)]
        )
    ]
    for load in loads:
        load.start()

    sent = []

    def send(src, dst, send_sem, recv_sem, device):
        copy = pltpu.make_async_remote_copy(
            src_ref=src, dst_ref=dst, send_sem=send_sem, recv_sem=recv_sem,
            device_id=device, device_id_type=MESH,
        )
        copy.start()
        sent.append(copy)
        return copy

    def send_x(level, xs, xr):
        return [
            send(xs.at[0:2], xr.at[0:2], xsend.at[level, 0], xrecv.at[level, 0], {"gx": right}),
            send(xs.at[2:4], xr.at[2:4], xsend.at[level, 1], xrecv.at[level, 1], {"gx": left}),
        ]

    def send_z(slot, zs, zr, groups):
        return [
            send(zs.at[0, groups], zr.at[0, groups], zsend.at[slot, 0], zrecv.at[slot, 0], {"gz": up}),
            send(zs.at[1, groups], zr.at[1, groups], zsend.at[slot, 1], zrecv.at[slot, 1], {"gz": down}),
        ]

    def send_rows(slot, at):
        return [
            send(zs1.at[d, 0, :, at], zr1.at[d, 0, :, at], zsend.at[slot, d], zrecv.at[slot, d], {"gz": k})
            for d, k in ((0, up), (1, down))
        ]

    units = [(g, k, r) for g in (1, 2, 3) for k in range(2) for r in range(2)]
    pending = list(units)
    on_way = {1: [], 2: [], 3: []}

    def send_units(count):
        for _ in range(min(count, len(pending))):
            g, k, r = pending.pop(0)
            at = pl.ds(32 * r, 32)
            for d, device in ((0, {"gz": up}), (1, {"gz": down})):
                i = units.index((g, k, r))
                on_way[g].append(
                    send(zs1.at[d, g, k, at], zr1.at[d, g, k, at], usend.at[i, d], urecv.at[i, d], device)
                )

    def arrive(copies):
        for copy in copies:
            copy.wait_recv()

    def x_split(y, xr, put):
        chunks, planes, half = y.shape[0], y.shape[1], y.shape[2] // 2
        wide = max(1, chunks // 2)

        def plane(p):
            for c in range(chunks):
                even = y[c, p, pl.ds(0, half, stride=2), :]
                odd = y[c, p, pl.ds(1, half, stride=2), :]
                if xr is None:
                    terms = [jnp.zeros((1, 128), jnp.float32)] * 4
                else:
                    terms = [xr[k, c, pl.ds(p, 1), :] for k in range(4)]
                low, high = lift_rows(even, odd, *terms)
                lanes = pl.ds(128 * (c % wide), 128)
                put(2 * (c // wide), p, lanes, low)
                put(2 * (c // wide) + 1, p, lanes, high)

        if planes == 8:
            lax.fori_loop(0, planes, lambda p, _: (plane(p), 0)[1], 0)
        else:
            for p in range(planes):
                plane(p)

    def into(own):
        def put(g, p, lanes, value):
            own[g, p, :, lanes] = value

        return put

    def z_terms(own, zs, groups, step):
        planes, rows = own.shape[1], own.shape[2]
        for g in groups:
            def chunk(i, _):
                at = pl.ds(pl.multiple_of(i * step, step), step)
                terms = edge_terms(lambda k: own[g, k, at, :], planes)
                for k in range(4):
                    zs[k // 2, g, k % 2, at, :] = terms[k]
                return 0

            lax.fori_loop(0, rows // step, chunk, 0)

    def z_split(own, zr, g, step, low_to, high_to):
        planes, rows = own.shape[1], own.shape[2]

        def chunk(i, _):
            at = pl.ds(pl.multiple_of(i * step, step), step)
            f = [own[g, k, at, :] for k in range(planes)]
            terms = [zr[k // 2, g, k % 2, at, :] for k in range(4)]
            low, high = lift_planes(f, *terms)
            for j in range(planes // 2):
                low_to[j, at, :] = low[j] * (KL * SCALE[g % 2])
                high_to[j, at, :] = high[j] * (KH * SCALE[g % 2])
            return 0

        lax.fori_loop(0, rows // step, chunk, 0)

    def bands(out, g):
        return out.at[2 * g - 1], out.at[2 * g]

    loads[1].wait()
    loads[0].wait()
    edges = edge_terms(lambda k: f1[:, k, :], f1.shape[1])
    out = lift_lanes(jnp.concatenate(edges, 0), pick[...])
    for k in range(4):
        for c in range(4):
            xs1[k, c] = out[c][8 * k : 8 * k + 8]

    def rows(i, _):
        at = pl.ds(pl.multiple_of(32 * i, 32), 32)
        terms = edge_terms(lambda k: f1[k, at, :], f1.shape[0])
        out = lift_lanes(jnp.concatenate(terms, 0), pick[...])
        for k in range(4):
            for c in range(4):
                yz1[c, k, at, :] = out[c][32 * k : 32 * k + 32]
        return 0

    lax.fori_loop(0, 4, rows, 0)
    pl.semaphore_wait(barrier, 6)
    x1 = send_x(0, xs1, xr1)

    def put_terms(g, p, lanes, value):
        zs1[p // 2, g, p % 2, :, lanes] = value

    x_split(yz1, None, put_terms)
    z1 = send_rows(0, pl.ds(8, 48))
    arrive(x1)
    for c in range(4):
        g, lanes = 2 * (c // 2), pl.ds(128 * (c % 2), 128)
        terms = [edge_terms(lambda i: xr1[k, c, i : i + 1, :], 8) for k in range(4)]
        for p in range(4):
            low, high = halo_effect(*(terms[k][p] for k in range(4)))
            for r, effect in zip((0, 1, 62, 63), low):
                zs1[p // 2, g, p % 2, r : r + 1, lanes] += effect
            for r, effect in zip((0, 62, 63), high):
                zs1[p // 2, g + 1, p % 2, r : r + 1, lanes] += effect
    z1 += send_rows(1, pl.ds(0, 8)) + send_rows(2, pl.ds(56, 8))
    send_units(4)

    def plane(p, _):
        out = lift_lanes(f1[p], pick[...])
        for c in range(4):
            y1[c, p] = out[c]
        return 0

    lax.fori_loop(0, f1.shape[0], plane, 0)
    x_split(y1, xr1, into(own1))

    arrive(z1)
    z_split(own1, zr1, 0, 8, f2, one.at[0])

    out = lift_lanes(f2[...].reshape(256, 256), pick[...])
    for c in range(2):
        y2[c] = out[c].reshape(4, 64, 128)
        for k, term in enumerate(edge_terms(lambda k: y2[c, :, k, :], 64)):
            xs2[k, c] = term
    x2 = send_x(1, xs2, xr2)
    send_units(3)
    arrive(x2)
    x_split(y2, xr2, into(own2))
    z_terms(own2, zs2, range(4), 32)
    z2 = send_z(3, zs2, zr2, 0)
    send_units(3)
    arrive(z2)
    z_split(own2, zr2, 0, 32, f3, two.at[0])

    loads[2].wait()
    y3[0] = dot(f3[...].reshape(64, 128), w3[...]).reshape(2, 32, 128)
    for k, term in enumerate(edge_terms(lambda k: y3[0, :, k, :], 32)):
        xs3[k, 0] = term
    x3 = send_x(2, xs3, xr3)
    send_units(2)
    arrive(x3)
    x_split(y3, xr3, into(own3))
    for xb in range(2):
        even, odd = own3[xb, 0], own3[xb, 1]
        a = odd + AL * even
        zs3[0, xb] = a
        zs3[1, xb] = even + BE * (AL * even + a)
        zs3[2, xb] = even
        zs3[3, xb] = even + BE * (odd + AL * even)
    z3 = [
        send(zs3.at[0:2], zr3.at[0:2], zsend.at[5, 0], zrecv.at[5, 0], {"gz": up}),
        send(zs3.at[2:4], zr3.at[2:4], zsend.at[5, 1], zrecv.at[5, 1], {"gz": down}),
        send(zs3.at[0:1], zr3b.at[0:1], zsend.at[6, 0], zrecv.at[6, 0], {"gz": up2}),
        send(zs3.at[2:3], zr3b.at[1:2], zsend.at[6, 1], zrecv.at[6, 1], {"gz": down2}),
    ]
    send_units(len(units))
    z2 = send_z(4, zs2, zr2, pl.ds(1, 3))
    for g in (1, 2):
        arrive(on_way[g])
        z_split(own1, zr1, g, 8, *bands(one, g))
    arrive(z3)
    for xb in range(2):
        a, b, e, c = (zr3[k, xb] for k in range(4))
        b = b + BE * zr3b[0, xb]
        c = c + (AL * BE) * zr3b[1, xb]
        low, high = lift_planes([own3[xb, 0], own3[xb, 1]], a, b, e, c)
        low, high = low[0] * (KL * SCALE[xb]), high[0] * (KH * SCALE[xb])
        for yb in range(2):
            lanes = slice(64 * yb, 64 * yb + 64)
            band = 2 * xb + 4 * yb
            if band == 0:
                coarse[0] = low[:, lanes]
            else:
                three[band - 1, 0] = low[:, lanes]
            three[band, 0] = high[:, lanes]
    arrive(on_way[3])
    z_split(own1, zr1, 3, 8, *bands(one, 3))
    arrive(z2)
    for g in (1, 2, 3):
        z_split(own2, zr2, g, 32, *bands(two, g))
    for copy in sent:
        copy.wait_send()


def place(one, two, three, coarse, one_to, two_to, three_to, coarse_to, sem):
    pairs = [(one.at[b], one_to.at[b]) for b in range(7)]
    pairs += [(two, two_to), (three, three_to), (coarse, coarse_to)]
    copies = [pltpu.make_async_copy(src, dst, sem.at[i]) for i, (src, dst) in enumerate(pairs)]
    for copy in copies:
        copy.start()
    for copy in copies:
        copy.wait()


def on_device(nz, nx, velocity):
    f32 = jnp.float32
    shapes = [(7, 4, 64, 256), (7, 2, 32, 128), (7, 1, 16, 64), (1, 16, 64)]
    scratch = [
        (8, 128, 512), None, (128, 128),
        (4, 8, 128, 128), (4, 4, 128, 128), (4, 4, 8, 128), (4, 4, 8, 128), (4, 8, 64, 256), (2, 4, 2, 64, 256), (2, 4, 2, 64, 256),
        (4, 64, 256), (2, 4, 64, 128), (4, 2, 4, 128), (4, 2, 4, 128), (4, 4, 32, 128), (2, 4, 2, 32, 128), (2, 4, 2, 32, 128),
        (2, 32, 128), (1, 2, 32, 128), (4, 1, 2, 128), (4, 1, 2, 128), (2, 2, 16, 128), (4, 2, 16, 128), (4, 2, 16, 128), (2, 2, 16, 128),
    ]
    dma = pltpu.SemaphoreType.DMA
    hbm = pl.BlockSpec(memory_space=pl.ANY)
    vmem = pl.BlockSpec(memory_space=pltpu.VMEM)
    results = pl.pallas_call(
        functools.partial(kernel, nz, nx),
        out_shape=tuple(pltpu.VMEM(s, f32) for s in shapes),
        in_specs=[hbm] * 3,
        out_specs=(vmem,) * 4,
        scratch_shapes=[pltpu.VMEM(s, f32) if s else pltpu.VMEM((256, 256), jnp.bfloat16) for s in scratch]
        + [dma((3,)), dma((3, 2)), dma((3, 2)), dma((7, 2)), dma((7, 2)), dma((12, 2)), dma((12, 2))],
        compiler_params=pltpu.CompilerParams(collective_id=0, has_side_effects=True),
        name="wavelet",
    )(velocity, jnp.asarray(deinterleave(256), jnp.bfloat16), jnp.asarray(band_matrix(128)))
    return pl.pallas_call(
        place,
        out_shape=tuple(jax.ShapeDtypeStruct(s, f32) for s in shapes),
        in_specs=[vmem] * 4,
        out_specs=(hbm,) * 4,
        scratch_shapes=[dma((10,))],
        name="place",
    )(*(pltpu.with_memory_space_constraint(r, pltpu.VMEM) for r in results))


def solution(mesh):
    return jax.shard_map(
        functools.partial(on_device, mesh.shape["gz"], mesh.shape["gx"]),
        mesh=mesh,
        in_specs=(P("gz", "gx", None),),
        out_specs=(
            P(None, "gz", "gx", None),
            P(None, "gz", "gx", None),
            P(None, "gz", "gx", None),
            P("gz", "gx", None),
        ),
        check_vma=False,
    )
```

```python
import functools

import jax
import jax.numpy as jnp
import numpy as np
from jax import lax
from jax.experimental import pallas as pl
from jax.experimental.pallas import tpu as pltpu
from jax.sharding import PartitionSpec as P

LOW_TAPS = (
    0.026748757411,
    -0.016864118443,
    -0.078223266529,
    0.266864118443,
    0.602949018236,
    0.266864118443,
    -0.078223266529,
    -0.016864118443,
    0.026748757411,
)
HIGH_TAPS = (
    0.091271763114,
    -0.057543526229,
    -0.591271763114,
    1.115087052457,
    -0.591271763114,
    -0.057543526229,
    0.091271763114,
)

AL = -1.586134342059924
BE = -0.052980118572961
GA = 0.882911075530934
DE = 0.443506852043971
KL = 1.0 / 1.230174104914001
KH = 1.230174104914001
SCALE = (KL, KH)

MESH = pl.DeviceIdType.MESH
HIGHEST = lax.Precision.HIGHEST


def band_matrix(n):
    half = n // 2
    w = np.zeros((n, n), np.float64)
    for j in range(half):
        for k in range(9):
            w[(2 * j + k - 4) % n, j] += LOW_TAPS[k]
        for k in range(7):
            w[(2 * j + 1 + k - 3) % n, half + j] += HIGH_TAPS[k]
    return w.astype(np.float32)


def edge_terms(get, n):
    a = get(n - 1) + AL * get(n - 2)
    b = get(n - 2) + BE * (get(n - 3) + AL * (get(n - 4) + get(n - 2)) + a)
    e = get(0)
    c = e + BE * (get(1) + AL * (e + get(2)))
    return a, b, e, c


def lift_planes(f, a, b, e_up, c):
    even, odd = f[0::2], f[1::2]
    n = len(even)
    even_next = even[1:] + [e_up]
    d1 = [odd[j] + AL * (even[j] + even_next[j]) for j in range(n)]
    d1m = a + AL * even[0]
    d1_prev = [d1m] + d1[:-1]
    s1 = [even[j] + BE * (d1_prev[j] + d1[j]) for j in range(n)]
    s1m = b + (AL * BE) * even[0]
    s1n = c + BE * d1[-1]
    s1_next = s1[1:] + [s1n]
    d2 = [d1[j] + GA * (s1[j] + s1_next[j]) for j in range(n)]
    d2m = d1m + GA * (s1m + s1[0])
    d2_prev = [d2m] + d2[:-1]
    s2 = [s1[j] + DE * (d2_prev[j] + d2[j]) for j in range(n)]
    return s2, d2


def from_above(x, row):
    n = x.shape[0]
    at = lax.broadcasted_iota(jnp.int32, x.shape, 0)
    return jnp.where(at == n - 1, row, pltpu.roll(x, n - 1, 0))


def from_below(x, row):
    at = lax.broadcasted_iota(jnp.int32, x.shape, 0)
    return jnp.where(at == 0, row, pltpu.roll(x, 1, 0))


def lift_rows(even, odd, a, b, e_up, c):
    n = even.shape[0]
    d1 = odd + AL * (even + from_above(even, e_up))
    d1m = a + AL * even[0:1]
    s1 = even + BE * (from_below(d1, d1m) + d1)
    s1m = b + (AL * BE) * even[0:1]
    s1n = c + BE * d1[n - 1 : n]
    d2 = d1 + GA * (s1 + from_above(s1, s1n))
    d2m = d1m + GA * (s1m + s1[0:1])
    s2 = s1 + DE * (from_below(d2, d2m) + d2)
    return s2, d2


def deinterleave(n):
    p = np.zeros((n, n), np.float32)
    for j in range(n // 2):
        p[2 * j, j] = p[2 * j + 1, n // 2 + j] = 1.0
    return p


def lift_lanes(x, pick):
    even, odd = [], []
    for b in range(x.shape[1] // 256):
        block = x[:, 256 * b : 256 * b + 256]
        parts = []
        for _ in range(3):
            parts.append(block.astype(jnp.bfloat16))
            block = block - parts[-1].astype(jnp.float32)
        out = sum(jnp.dot(part, pick, preferred_element_type=jnp.float32) for part in parts)
        even.append(out[:, :128])
        odd.append(out[:, 128:])
    n = len(even)
    lane = lax.broadcasted_iota(jnp.int32, even[0].shape, 1)

    def following(v):
        moved = [pltpu.roll(u, 127, 1) for u in v]
        return moved if n == 1 else [jnp.where(lane == 127, moved[(i + 1) % n], moved[i]) for i in range(n)]

    def preceding(v):
        moved = [pltpu.roll(u, 1, 1) for u in v]
        return moved if n == 1 else [jnp.where(lane == 0, moved[(i - 1) % n], moved[i]) for i in range(n)]

    def step(v, factor, w, shifted):
        return [p + factor * (q + r) for p, q, r in zip(v, w, shifted(w))]

    d1 = step(odd, AL, even, following)
    s1 = step(even, BE, d1, preceding)
    d2 = step(d1, GA, s1, following)
    s2 = step(s1, DE, d2, preceding)
    return [KL * u for u in s2] + [KH * u for u in d2]


def halo_effect(a, b, e, c):
    first = (GA * BE) * a
    before = a + GA * (b + BE * a)
    q = AL * e
    last = q + GA * (c + (2 * BE) * q)
    last_but = (GA * BE) * q
    low = (BE * a + DE * (before + first), DE * first, DE * last_but, BE * q + DE * (last_but + last))
    return low, (first, last_but, last)


def dot(x, w):
    return jnp.dot(x, w, precision=HIGHEST, preferred_element_type=jnp.float32)


def kernel(
    nz, nx,
    v_hbm, pick_hbm, w3_hbm,
    one, two, three, coarse,
    f1, pick, w3, y1, yz1, xz1, xs1, xr1, own1, zs1, zr1,
    f2, y2, xs2, xr2, own2, zs2, zr2,
    f3, y3, xs3, xr3, own3, zs3, zr3, zr3b,
    in_sem, xsend, xrecv, zsend, zrecv, usend, urecv,
):
    iz, ix = lax.axis_index("gz"), lax.axis_index("gx")
    right, left = lax.rem(ix + 1, nx), lax.rem(ix + nx - 1, nx)
    up, down = lax.rem(iz + 1, nz), lax.rem(iz + nz - 1, nz)
    up2, down2 = lax.rem(iz + 2, nz), lax.rem(iz + nz - 2, nz)

    near = lax.rem(iz, 2)
    sides = [(d, {"gz": lax.rem(iz + nz + 1 - 2 * d, nz)}) for d in (1 - near, near)]

    barrier = pltpu.get_barrier_semaphore()
    for k in (right, left):
        pl.semaphore_signal(barrier, inc=1, device_id={"gx": k}, device_id_type=MESH)
    for k in (up, down, up2, down2):
        pl.semaphore_signal(barrier, inc=1, device_id={"gz": k}, device_id_type=MESH)

    parts = (0, 3, 1, 2)
    loads = [
        pltpu.make_async_copy(v_hbm.at[:, pl.ds(32 * k, 32)], f1.at[:, pl.ds(32 * k, 32)], in_sem.at[i])
        for i, k in enumerate(parts)
    ]
    loads += [
        pltpu.make_async_copy(src, dst, in_sem.at[i]) for i, src, dst in ((4, pick_hbm, pick), (5, w3_hbm, w3))
    ]
    for load in loads:
        load.start()

    sent = []

    def send(src, dst, send_sem, recv_sem, device):
        copy = pltpu.make_async_remote_copy(
            src_ref=src, dst_ref=dst, send_sem=send_sem, recv_sem=recv_sem,
            device_id=device, device_id_type=MESH,
        )
        copy.start()
        sent.append(copy)
        return copy

    def send_x(level, xs, xr):
        return [
            send(xs.at[0:2], xr.at[0:2], xsend.at[level, 0], xrecv.at[level, 0], {"gx": right}),
            send(xs.at[2:4], xr.at[2:4], xsend.at[level, 1], xrecv.at[level, 1], {"gx": left}),
        ]

    def send_z(slot, zs, zr, *at, which=(0, 1)):
        return [
            send(zs.at[(d,) + at], zr.at[(d,) + at], zsend.at[slot, d], zrecv.at[slot, d], device)
            for d, device in (sides[w] for w in which)
        ]

    units = [(g, k, r) for g in (1, 2, 3) for k in range(2) for r in range(2)]
    pending = list(units)
    on_way = {1: [], 2: [], 3: []}

    def send_units(count, which=(0, 1)):
        done = len(units) - len(pending)
        for i in range(done, done + count):
            g, k, r = units[i]
            at = pl.ds(32 * r, 32)
            for d, device in (sides[w] for w in which):
                on_way[g].append(
                    send(zs1.at[d, g, k, at], zr1.at[d, g, k, at], usend.at[i, d], urecv.at[i, d], device)
                )
        if which[-1] == 1:
            del pending[:count]

    def arrive(copies):
        for copy in copies:
            copy.wait_recv()

    def x_split(y, xr, put):
        chunks, planes, half = y.shape[0], y.shape[1], y.shape[2] // 2

        def plane(p):
            for c in range(chunks):
                even = y[c, p, pl.ds(0, half, stride=2), :]
                odd = y[c, p, pl.ds(1, half, stride=2), :]
                if xr is None:
                    terms = [jnp.zeros((1, 128), jnp.float32)] * 4
                else:
                    terms = [xr[k, c, pl.ds(p, 1), :] for k in range(4)]
                low, high = lift_rows(even, odd, *terms)
                put(c, 0, p, low)
                put(c, 1, p, high)

        if planes == 8:
            lax.fori_loop(0, planes // 2, lambda i, _: (plane(2 * i), plane(2 * i + 1), 0)[2], 0)
        else:
            for p in range(planes):
                plane(p)

    def into(own, wide):
        def put(c, xb, p, value):
            own[2 * (c // wide) + xb, p, :, pl.ds(128 * (c % wide), 128)] = value

        return put

    def z_terms(own, zs, groups, step):
        planes, rows = own.shape[1], own.shape[2]
        for g in groups:
            def chunk(i, _):
                at = pl.ds(pl.multiple_of(i * step, step), step)
                terms = edge_terms(lambda k: own[g, k, at, :], planes)
                for k in range(4):
                    zs[k // 2, g, k % 2, at, :] = terms[k]
                return 0

            lax.fori_loop(0, rows // step, chunk, 0)

    def z_split(own, zr, g, step, low_to, high_to):
        planes, rows = own.shape[1], own.shape[2]

        def chunk(i, _):
            at = pl.ds(pl.multiple_of(i * step, step), step)
            f = [own[g, k, at, :] for k in range(planes)]
            terms = [zr[k // 2, g, k % 2, at, :] for k in range(4)]
            low, high = lift_planes(f, *terms)
            for j in range(planes // 2):
                low_to[j, at, :] = low[j] * (KL * SCALE[g % 2])
                high_to[j, at, :] = high[j] * (KH * SCALE[g % 2])
            return 0

        lax.fori_loop(0, rows // step, chunk, 0)

    def bands(out, g):
        return out.at[2 * g - 1], out.at[2 * g]

    for i, part in enumerate(parts):
        loads[i].wait()
        at = pl.ds(32 * part, 32)
        for c in range(4):
            terms = edge_terms(lambda k: f1[k, at, pl.ds(128 * c, 128)], f1.shape[0])
            for k in range(4):
                yz1[c, k, at, :] = terms[k]

    def put_raw(c, xb, p, value):
        xz1[xb, p, :, pl.ds(128 * c, 128)] = value

    x_split(yz1, None, put_raw)
    edges = edge_terms(lambda k: f1[:, k, :], f1.shape[1])
    loads[4].wait()

    def put_terms(xb, out):
        for c in range(4):
            for p in range(4):
                zs1[p // 2, 2 * (c // 2) + xb, p % 2, :, pl.ds(128 * (c % 2), 128)] = out[c][64 * p : 64 * p + 64]

    out = lift_lanes(jnp.concatenate([xz1[0].reshape(256, 512), *edges], 0), pick[...])
    for k in range(4):
        for c in range(4):
            xs1[k, c] = out[c][256 + 8 * k : 264 + 8 * k]
    put_terms(0, out)
    pl.semaphore_wait(barrier, 6)
    x1 = send_x(0, xs1, xr1)
    z1 = send_z(0, zs1, zr1, 0, slice(None), pl.ds(8, 48))
    put_terms(1, lift_lanes(xz1[1].reshape(256, 512), pick[...]))

    def rows(i, _):
        at = pl.ds(2 * i, 2)
        out = lift_lanes(f1[at].reshape(256, 512), pick[...])
        for c in range(4):
            y1[c, at] = out[c].reshape(2, 128, 128)
        return 0

    lax.fori_loop(0, f1.shape[0] // 2, rows, 0)

    arrive(x1)
    for c in range(4):
        g, lanes = 2 * (c // 2), pl.ds(128 * (c % 2), 128)
        terms = [edge_terms(lambda i: xr1[k, c, i : i + 1, :], 8) for k in range(4)]
        for p in range(4):
            low, high = halo_effect(*(terms[k][p] for k in range(4)))
            for r, effect in zip((0, 1, 62, 63), low):
                zs1[p // 2, g, p % 2, r : r + 1, lanes] += effect
            for r, effect in zip((0, 62, 63), high):
                zs1[p // 2, g + 1, p % 2, r : r + 1, lanes] += effect
    z1 += send_z(1, zs1, zr1, 0, slice(None), pl.ds(0, 8)) + send_z(2, zs1, zr1, 0, slice(None), pl.ds(56, 8))
    send_units(3)
    x_split(y1, xr1, into(own1, 2))

    arrive(z1)
    z_split(own1, zr1, 0, 8, f2, one.at[0])

    out = lift_lanes(f2[...].reshape(256, 256), pick[...])
    for c in range(2):
        y2[c] = out[c].reshape(4, 64, 128)
        for k, term in enumerate(edge_terms(lambda k: y2[c, :, k, :], 64)):
            xs2[k, c] = term
    x2 = send_x(1, xs2, xr2)
    send_units(3)
    arrive(x2)
    x_split(y2, xr2, into(own2, 1))
    z_terms(own2, zs2, range(4), 32)
    z2 = send_z(3, zs2, zr2, 0)
    send_units(3)
    arrive(z2)
    z_split(own2, zr2, 0, 32, f3, two.at[0])

    loads[5].wait()
    y3[0] = dot(f3[...].reshape(64, 128), w3[...]).reshape(2, 32, 128)
    for k, term in enumerate(edge_terms(lambda k: y3[0, :, k, :], 32)):
        xs3[k, 0] = term
    x3 = send_x(2, xs3, xr3)
    send_units(2)
    arrive(x3)
    x_split(y3, xr3, into(own3, 1))
    for xb in range(2):
        even, odd = own3[xb, 0], own3[xb, 1]
        a = odd + AL * even
        zs3[0, xb] = a
        zs3[1, xb] = even + BE * (AL * even + a)
        zs3[2, xb] = even
        zs3[3, xb] = even + BE * (odd + AL * even)
    z3 = [
        send(zs3.at[0:2], zr3.at[0:2], zsend.at[5, 0], zrecv.at[5, 0], {"gz": up}),
        send(zs3.at[2:4], zr3.at[2:4], zsend.at[5, 1], zrecv.at[5, 1], {"gz": down}),
        send(zs3.at[0:1], zr3b.at[0:1], zsend.at[6, 0], zrecv.at[6, 0], {"gz": up2}),
        send(zs3.at[2:3], zr3b.at[1:2], zsend.at[6, 1], zrecv.at[6, 1], {"gz": down2}),
    ]
    z2 = []
    for w in range(2):
        send_units(1, (w,))
        z2 += send_z(4, zs2, zr2, pl.ds(1, 3), which=(w,))
    for g in (1, 2):
        arrive(on_way[g])
        z_split(own1, zr1, g, 8, *bands(one, g))
    arrive(z3)
    for xb in range(2):
        a, b, e, c = (zr3[k, xb] for k in range(4))
        b = b + BE * zr3b[0, xb]
        c = c + (AL * BE) * zr3b[1, xb]
        low, high = lift_planes([own3[xb, 0], own3[xb, 1]], a, b, e, c)
        low, high = low[0] * (KL * SCALE[xb]), high[0] * (KH * SCALE[xb])
        for yb in range(2):
            lanes = slice(64 * yb, 64 * yb + 64)
            band = 2 * xb + 4 * yb
            if band == 0:
                coarse[0] = low[:, lanes]
            else:
                three[band - 1, 0] = low[:, lanes]
            three[band, 0] = high[:, lanes]
    arrive(on_way[3])
    z_split(own1, zr1, 3, 8, *bands(one, 3))
    arrive(z2)
    for g in (1, 2, 3):
        z_split(own2, zr2, g, 32, *bands(two, g))
    for copy in sent:
        copy.wait_send()


def place(one, two, three, coarse, one_to, two_to, three_to, coarse_to, sem):
    pairs = [(one.at[b], one_to.at[b]) for b in range(7)]
    pairs += [(two, two_to), (three, three_to), (coarse, coarse_to)]
    copies = [pltpu.make_async_copy(src, dst, sem.at[i]) for i, (src, dst) in enumerate(pairs)]
    for copy in copies:
        copy.start()
    for copy in copies:
        copy.wait()


def on_device(nz, nx, velocity):
    f32 = jnp.float32
    shapes = [(7, 4, 64, 256), (7, 2, 32, 128), (7, 1, 16, 64), (1, 16, 64)]
    scratch = [
        (8, 128, 512), None, (128, 128),
        (4, 8, 128, 128), (4, 4, 128, 128), (2, 4, 64, 512), (4, 4, 8, 128), (4, 4, 8, 128), (4, 8, 64, 256), (2, 4, 2, 64, 256), (2, 4, 2, 64, 256),
        (4, 64, 256), (2, 4, 64, 128), (4, 2, 4, 128), (4, 2, 4, 128), (4, 4, 32, 128), (2, 4, 2, 32, 128), (2, 4, 2, 32, 128),
        (2, 32, 128), (1, 2, 32, 128), (4, 1, 2, 128), (4, 1, 2, 128), (2, 2, 16, 128), (4, 2, 16, 128), (4, 2, 16, 128), (2, 2, 16, 128),
    ]
    dma = pltpu.SemaphoreType.DMA
    hbm = pl.BlockSpec(memory_space=pl.ANY)
    vmem = pl.BlockSpec(memory_space=pltpu.VMEM)
    results = pl.pallas_call(
        functools.partial(kernel, nz, nx),
        out_shape=tuple(pltpu.VMEM(s, f32) for s in shapes),
        in_specs=[hbm] * 3,
        out_specs=(vmem,) * 4,
        scratch_shapes=[pltpu.VMEM(s, f32) if s else pltpu.VMEM((256, 256), jnp.bfloat16) for s in scratch]
        + [dma((6,)), dma((3, 2)), dma((3, 2)), dma((7, 2)), dma((7, 2)), dma((12, 2)), dma((12, 2))],
        compiler_params=pltpu.CompilerParams(collective_id=0, has_side_effects=True),
        name="wavelet",
    )(velocity, jnp.asarray(deinterleave(256), jnp.bfloat16), jnp.asarray(band_matrix(128)))
    return pl.pallas_call(
        place,
        out_shape=tuple(jax.ShapeDtypeStruct(s, f32) for s in shapes),
        in_specs=[vmem] * 4,
        out_specs=(hbm,) * 4,
        scratch_shapes=[dma((10,))],
        name="place",
    )(*(pltpu.with_memory_space_constraint(r, pltpu.VMEM) for r in results))


def solution(mesh):
    return jax.shard_map(
        functools.partial(on_device, mesh.shape["gz"], mesh.shape["gx"]),
        mesh=mesh,
        in_specs=(P("gz", "gx", None),),
        out_specs=(
            P(None, "gz", "gx", None),
            P(None, "gz", "gx", None),
            P(None, "gz", "gx", None),
            P("gz", "gx", None),
        ),
        check_vma=False,
    )
```

```python
import functools

import jax
import jax.numpy as jnp
import numpy as np
from jax import lax
from jax.experimental import pallas as pl
from jax.experimental.pallas import tpu as pltpu
from jax.sharding import PartitionSpec as P

LOW_TAPS = (
    0.026748757411,
    -0.016864118443,
    -0.078223266529,
    0.266864118443,
    0.602949018236,
    0.266864118443,
    -0.078223266529,
    -0.016864118443,
    0.026748757411,
)
HIGH_TAPS = (
    0.091271763114,
    -0.057543526229,
    -0.591271763114,
    1.115087052457,
    -0.591271763114,
    -0.057543526229,
    0.091271763114,
)

AL = -1.586134342059924
BE = -0.052980118572961
GA = 0.882911075530934
DE = 0.443506852043971
KL = 1.0 / 1.230174104914001
KH = 1.230174104914001
SCALE = (KL, KH)

UNITS = (4, 3, 3, 2)

MESH = pl.DeviceIdType.MESH
HIGHEST = lax.Precision.HIGHEST


def band_matrix(n):
    half = n // 2
    w = np.zeros((n, n), np.float64)
    for j in range(half):
        for k in range(9):
            w[(2 * j + k - 4) % n, j] += LOW_TAPS[k]
        for k in range(7):
            w[(2 * j + 1 + k - 3) % n, half + j] += HIGH_TAPS[k]
    return w.astype(np.float32)


def edge_terms(get, n):
    a = get(n - 1) + AL * get(n - 2)
    b = get(n - 2) + BE * (get(n - 3) + AL * (get(n - 4) + get(n - 2)) + a)
    e = get(0)
    c = e + BE * (get(1) + AL * (e + get(2)))
    return a, b, e, c


def lift_planes(f, a, b, e_up, c):
    even, odd = f[0::2], f[1::2]
    n = len(even)
    even_next = even[1:] + [e_up]
    d1 = [odd[j] + AL * (even[j] + even_next[j]) for j in range(n)]
    d1m = a + AL * even[0]
    d1_prev = [d1m] + d1[:-1]
    s1 = [even[j] + BE * (d1_prev[j] + d1[j]) for j in range(n)]
    s1m = b + (AL * BE) * even[0]
    s1n = c + BE * d1[-1]
    s1_next = s1[1:] + [s1n]
    d2 = [d1[j] + GA * (s1[j] + s1_next[j]) for j in range(n)]
    d2m = d1m + GA * (s1m + s1[0])
    d2_prev = [d2m] + d2[:-1]
    s2 = [s1[j] + DE * (d2_prev[j] + d2[j]) for j in range(n)]
    return s2, d2


def from_above(x, row):
    n = x.shape[0]
    at = lax.broadcasted_iota(jnp.int32, x.shape, 0)
    return jnp.where(at == n - 1, row, pltpu.roll(x, n - 1, 0))


def from_below(x, row):
    at = lax.broadcasted_iota(jnp.int32, x.shape, 0)
    return jnp.where(at == 0, row, pltpu.roll(x, 1, 0))


def lift_rows(even, odd, a, b, e_up, c):
    n = even.shape[0]
    d1 = odd + AL * (even + from_above(even, e_up))
    d1m = a + AL * even[0:1]
    s1 = even + BE * (from_below(d1, d1m) + d1)
    s1m = b + (AL * BE) * even[0:1]
    s1n = c + BE * d1[n - 1 : n]
    d2 = d1 + GA * (s1 + from_above(s1, s1n))
    d2m = d1m + GA * (s1m + s1[0:1])
    s2 = s1 + DE * (from_below(d2, d2m) + d2)
    return s2, d2


def deinterleave(n):
    p = np.zeros((n, n), np.float32)
    for j in range(n // 2):
        p[2 * j, j] = p[2 * j + 1, n // 2 + j] = 1.0
    return p


def lift_lanes(x, pick):
    even, odd = [], []
    for b in range(x.shape[1] // 256):
        block = x[:, 256 * b : 256 * b + 256]
        parts = []
        for _ in range(3):
            parts.append(block.astype(jnp.bfloat16))
            block = block - parts[-1].astype(jnp.float32)
        out = sum(jnp.dot(part, pick, preferred_element_type=jnp.float32) for part in parts)
        even.append(out[:, :128])
        odd.append(out[:, 128:])
    n = len(even)
    lane = lax.broadcasted_iota(jnp.int32, even[0].shape, 1)

    def following(v):
        moved = [pltpu.roll(u, 127, 1) for u in v]
        return moved if n == 1 else [jnp.where(lane == 127, moved[(i + 1) % n], moved[i]) for i in range(n)]

    def preceding(v):
        moved = [pltpu.roll(u, 1, 1) for u in v]
        return moved if n == 1 else [jnp.where(lane == 0, moved[(i - 1) % n], moved[i]) for i in range(n)]

    def step(v, factor, w, shifted):
        return [p + factor * (q + r) for p, q, r in zip(v, w, shifted(w))]

    d1 = step(odd, AL, even, following)
    s1 = step(even, BE, d1, preceding)
    d2 = step(d1, GA, s1, following)
    s2 = step(s1, DE, d2, preceding)
    return [KL * u for u in s2] + [KH * u for u in d2]


def halo_effect(a, b, e, c):
    first = (GA * BE) * a
    before = a + GA * (b + BE * a)
    q = AL * e
    last = q + GA * (c + (2 * BE) * q)
    last_but = (GA * BE) * q
    low = (BE * a + DE * (before + first), DE * first, DE * last_but, BE * q + DE * (last_but + last))
    return low, (first, last_but, last)


def dot(x, w):
    return jnp.dot(x, w, precision=HIGHEST, preferred_element_type=jnp.float32)


def kernel(
    nz, nx,
    v_hbm, pick_hbm, w3_hbm,
    one, two, three, coarse,
    f1, pick, w3, y1, yz1, xz1, xs1, xr1, own1, zs1, zr1,
    f2, y2, yz2, xs2, xr2, cs2, cr2, own2, zs2, zr2,
    f3, y3, yz3, xs3, xr3, cs3, cr3, cr3b, own3, zs3, zr3, zr3b,
    in_sem, xsend, xrecv, csend, crecv, zsend, zrecv, usend, urecv,
):
    iz, ix = lax.axis_index("gz"), lax.axis_index("gx")
    right, left = lax.rem(ix + 1, nx), lax.rem(ix + nx - 1, nx)
    up, down = lax.rem(iz + 1, nz), lax.rem(iz + nz - 1, nz)
    up2, down2 = lax.rem(iz + 2, nz), lax.rem(iz + nz - 2, nz)

    near = lax.rem(iz, 2)
    sides = [(d, {"gz": lax.rem(iz + nz + 1 - 2 * d, nz)}) for d in (1 - near, near)]

    barrier = pltpu.get_barrier_semaphore()
    others = [{"gx": k} for k in (right, left)]
    for k in (up, down, up2, down2):
        others += [{"gz": k}, {"gz": k, "gx": right}, {"gz": k, "gx": left}]
    for k in others:
        pl.semaphore_signal(barrier, inc=1, device_id=k, device_id_type=MESH)

    parts = (0, 3, 1, 2)
    loads = [
        pltpu.make_async_copy(v_hbm.at[:, pl.ds(32 * k, 32)], f1.at[:, pl.ds(32 * k, 32)], in_sem.at[i])
        for i, k in enumerate(parts)
    ]
    loads += [
        pltpu.make_async_copy(src, dst, in_sem.at[i]) for i, src, dst in ((4, pick_hbm, pick), (5, w3_hbm, w3))
    ]
    for load in loads:
        load.start()

    sent = []

    def send(src, dst, send_sem, recv_sem, device):
        copy = pltpu.make_async_remote_copy(
            src_ref=src, dst_ref=dst, send_sem=send_sem, recv_sem=recv_sem,
            device_id=device, device_id_type=MESH,
        )
        copy.start()
        sent.append(copy)
        return copy

    def send_x(level, xs, xr):
        return [
            send(xs.at[0:2], xr.at[0:2], xsend.at[level, 0], xrecv.at[level, 0], {"gx": right}),
            send(xs.at[2:4], xr.at[2:4], xsend.at[level, 1], xrecv.at[level, 1], {"gx": left}),
        ]

    def send_z(slot, zs, zr, *at, which=(0, 1)):
        return [
            send(zs.at[(d,) + at], zr.at[(d,) + at], zsend.at[slot, d], zrecv.at[slot, d], device)
            for d, device in (sides[w] for w in which)
        ]

    def send_corners(slot, cs, cr, above, below):
        return [
            send(cs.at[d, h], cr.at[d, h], csend.at[slot, d, h], crecv.at[slot, d, h], {"gz": k, "gx": m})
            for d, k in ((0, above), (1, below))
            for h, m in ((0, right), (1, left))
        ]

    units = [(g, k, r) for g in (1, 2, 3) for k in range(2) for r in range(2)]
    pending = list(units)
    on_way = {1: [], 2: [], 3: []}

    def send_units(count, which=(0, 1)):
        done = len(units) - len(pending)
        for i in range(done, done + count):
            g, k, r = units[i]
            at = pl.ds(32 * r, 32)
            for d, device in (sides[w] for w in which):
                on_way[g].append(
                    send(zs1.at[d, g, k, at], zr1.at[d, g, k, at], usend.at[i, d], urecv.at[i, d], device)
                )
        if which[-1] == 1:
            del pending[:count]

    def arrive(copies):
        for copy in copies:
            copy.wait_recv()

    def x_split(y, xr, put):
        chunks, planes, half = y.shape[0], y.shape[1], y.shape[2] // 2

        def plane(p):
            for c in range(chunks):
                even = y[c, p, pl.ds(0, half, stride=2), :]
                odd = y[c, p, pl.ds(1, half, stride=2), :]
                if xr is None:
                    terms = [jnp.zeros((1, 128), jnp.float32)] * 4
                else:
                    terms = [xr[k, c, pl.ds(p, 1), :] for k in range(4)]
                low, high = lift_rows(even, odd, *terms)
                put(c, 0, p, low)
                put(c, 1, p, high)

        if planes == 8:
            lax.fori_loop(0, planes // 2, lambda i, _: (plane(2 * i), plane(2 * i + 1), 0)[2], 0)
        else:
            for p in range(planes):
                plane(p)

    def into(own, wide):
        def put(c, xb, p, value):
            own[2 * (c // wide) + xb, p, :, pl.ds(128 * (c % wide), 128)] = value

        return put

    def z_split(own, zr, g, step, low_to, high_to):
        planes, rows = own.shape[1], own.shape[2]

        def chunk(i, _):
            at = pl.ds(pl.multiple_of(i * step, step), step)
            f = [own[g, k, at, :] for k in range(planes)]
            terms = [zr[k // 2, g, k % 2, at, :] for k in range(4)]
            low, high = lift_planes(f, *terms)
            for j in range(planes // 2):
                low_to[j, at, :] = low[j] * (KL * SCALE[g % 2])
                high_to[j, at, :] = high[j] * (KH * SCALE[g % 2])
            return 0

        lax.fori_loop(0, rows // step, chunk, 0)

    def bands(out, g):
        return out.at[2 * g - 1], out.at[2 * g]

    for i, part in enumerate(parts):
        loads[i].wait()
        at = pl.ds(32 * part, 32)
        for c in range(4):
            terms = edge_terms(lambda k: f1[k, at, pl.ds(128 * c, 128)], f1.shape[0])
            for k in range(4):
                yz1[c, k, at, :] = terms[k]

    def put_raw(c, xb, p, value):
        xz1[xb, p, :, pl.ds(128 * c, 128)] = value

    x_split(yz1, None, put_raw)
    edges = edge_terms(lambda k: f1[:, k, :], f1.shape[1])
    loads[4].wait()

    def put_terms(xb, out):
        for c in range(4):
            for p in range(4):
                zs1[p // 2, 2 * (c // 2) + xb, p % 2, :, pl.ds(128 * (c % 2), 128)] = out[c][64 * p : 64 * p + 64]

    out = lift_lanes(jnp.concatenate([xz1[0].reshape(256, 512), *edges], 0), pick[...])
    for k in range(4):
        for c in range(4):
            xs1[k, c] = out[c][256 + 8 * k : 264 + 8 * k]
    put_terms(0, out)
    pl.semaphore_wait(barrier, len(others))
    x1 = send_x(0, xs1, xr1)
    z1 = send_z(0, zs1, zr1, 0, slice(None), pl.ds(8, 48))
    put_terms(1, lift_lanes(xz1[1].reshape(256, 512), pick[...]))

    def rows(i, _):
        at = pl.ds(2 * i, 2)
        out = lift_lanes(f1[at].reshape(256, 512), pick[...])
        for c in range(4):
            y1[c, at] = out[c].reshape(2, 128, 128)
        return 0

    lax.fori_loop(0, f1.shape[0] // 2, rows, 0)

    arrive(x1)
    for c in range(4):
        g, lanes = 2 * (c // 2), pl.ds(128 * (c % 2), 128)
        terms = [edge_terms(lambda i: xr1[k, c, i : i + 1, :], 8) for k in range(4)]
        for p in range(4):
            low, high = halo_effect(*(terms[k][p] for k in range(4)))
            for r, effect in zip((0, 1, 62, 63), low):
                zs1[p // 2, g, p % 2, r : r + 1, lanes] += effect
            for r, effect in zip((0, 62, 63), high):
                zs1[p // 2, g + 1, p % 2, r : r + 1, lanes] += effect
    z1 += send_z(1, zs1, zr1, 0, slice(None), pl.ds(0, 8)) + send_z(2, zs1, zr1, 0, slice(None), pl.ds(56, 8))
    send_units(UNITS[0])
    x_split(y1, xr1, into(own1, 2))

    arrive(z1)
    z_split(own1, zr1, 0, 8, f2, one.at[0])

    def add_halo(to, terms, wanted):
        low, high = halo_effect(*terms)
        n = to(0).shape[0]
        if 0 in wanted:
            for r, effect in zip((0, 1, n - 2, n - 1), low):
                to(0)[r : r + 1, :] += effect
        if 1 in wanted:
            for r, effect in zip((0, n - 2, n - 1), high):
                to(1)[r : r + 1, :] += effect

    out = lift_lanes(f2[...].reshape(256, 256), pick[...])
    for c in range(2):
        y2[c] = out[c].reshape(4, 64, 128)
        for k, term in enumerate(edge_terms(lambda k: y2[c, :, k, :], 64)):
            xs2[k, c] = term
        for k, term in enumerate(edge_terms(lambda k: y2[c, k], 4)):
            yz2[c, k] = term
        for t in range(4):
            for k, term in enumerate(edge_terms(lambda i: xs2[t, c, i : i + 1, :], 4)):
                cs2[k // 2, t // 2, k % 2, t % 2, c : c + 1, :] = term

    def put_terms2(c, xb, p, value):
        zs2[p // 2, 2 * c + xb, p % 2] = value

    x2 = send_x(1, xs2, xr2) + send_corners(0, cs2, cr2, up, down)
    x_split(yz2, None, put_terms2)
    z2 = send_z(3, zs2, zr2, 0)
    send_units(UNITS[1])

    def add_halo2(c, wanted):
        for d in range(2):
            for k in range(2):
                add_halo(
                    lambda xb: zr2.at[d, 2 * c + xb, k],
                    [cr2[d, t // 2, k, t % 2, c : c + 1, :] for t in range(4)],
                    wanted,
                )

    arrive(x2)
    x_split(y2, xr2, into(own2, 1))
    arrive(z2)
    add_halo2(0, (0,))
    z_split(own2, zr2, 0, 32, f3, two.at[0])

    def terms3(even, odd):
        a = odd + AL * even
        return a, even + BE * (AL * even + a), even, even + BE * a

    loads[5].wait()
    y3[0] = dot(f3[...].reshape(64, 128), w3[...]).reshape(2, 32, 128)
    for k, term in enumerate(edge_terms(lambda k: y3[0, :, k, :], 32)):
        xs3[k, 0] = term
    for k, term in enumerate(terms3(y3[0, 0], y3[0, 1])):
        yz3[0, k] = term
    for t in range(4):
        for k, term in enumerate(terms3(xs3[t, 0, 0:1, :], xs3[t, 0, 1:2, :])):
            cs3[k // 2, t // 2, k % 2, t % 2 : t % 2 + 1, :] = term

    def put_terms3(c, xb, p, value):
        zs3[p // 2, p % 2, xb] = value

    x3 = send_x(2, xs3, xr3) + send_corners(1, cs3, cr3, up, down)
    x3 += [
        send(cs3.at[d, h, 0], cr3b.at[d, h], csend.at[2, d, h], crecv.at[2, d, h], {"gz": k, "gx": m})
        for d, k in ((0, up2), (1, down2))
        for h, m in ((0, right), (1, left))
    ]
    x_split(yz3, None, put_terms3)
    z3 = send_z(5, zs3, zr3)
    z3 += [
        send(zs3.at[d, 0], zr3b.at[d], zsend.at[6, d], zrecv.at[6, d], {"gz": k})
        for d, k in ((0, up2), (1, down2))
    ]
    send_units(UNITS[2])
    z2 = send_z(4, zs2, zr2, pl.ds(1, 3))
    for w in range(2):
        send_units(UNITS[3], (w,))

    arrive(x3)
    x_split(y3, xr3, into(own3, 1))
    arrive(z3)
    for d in range(2):
        for k in range(2):
            add_halo(lambda xb: zr3.at[d, k, xb], [cr3[d, t // 2, k, t % 2 : t % 2 + 1, :] for t in range(4)], (0, 1))
        add_halo(lambda xb: zr3b.at[d, xb], [cr3b[d, t // 2, t % 2 : t % 2 + 1, :] for t in range(4)], (0, 1))
    for xb in range(2):
        a, b, e, c = (zr3[k // 2, k % 2, xb] for k in range(4))
        b = b + BE * zr3b[0, xb]
        c = c + (AL * BE) * zr3b[1, xb]
        low, high = lift_planes([own3[xb, 0], own3[xb, 1]], a, b, e, c)
        low, high = low[0] * (KL * SCALE[xb]), high[0] * (KH * SCALE[xb])
        for yb in range(2):
            lanes = slice(64 * yb, 64 * yb + 64)
            band = 2 * xb + 4 * yb
            if band == 0:
                coarse[0] = low[:, lanes]
            else:
                three[band - 1, 0] = low[:, lanes]
            three[band, 0] = high[:, lanes]

    for g in (1, 2):
        arrive(on_way[g])
        z_split(own1, zr1, g, 8, *bands(one, g))
    arrive(z2)
    add_halo2(0, (1,))
    add_halo2(1, (0, 1))
    for g in (1, 2, 3):
        z_split(own2, zr2, g, 32, *bands(two, g))
    arrive(on_way[3])
    z_split(own1, zr1, 3, 8, *bands(one, 3))
    for copy in sent:
        copy.wait_send()


def place(one, two, three, coarse, one_to, two_to, three_to, coarse_to, sem):
    pairs = [(one.at[b], one_to.at[b]) for b in range(7)]
    pairs += [(two, two_to), (three, three_to), (coarse, coarse_to)]
    copies = [pltpu.make_async_copy(src, dst, sem.at[i]) for i, (src, dst) in enumerate(pairs)]
    for copy in copies:
        copy.start()
    for copy in copies:
        copy.wait()


def on_device(nz, nx, velocity):
    f32 = jnp.float32
    shapes = [(7, 4, 64, 256), (7, 2, 32, 128), (7, 1, 16, 64), (1, 16, 64)]
    scratch = [
        (8, 128, 512), None, (128, 128),
        (4, 8, 128, 128), (4, 4, 128, 128), (2, 4, 64, 512), (4, 4, 8, 128), (4, 4, 8, 128), (4, 8, 64, 256), (2, 4, 2, 64, 256), (2, 4, 2, 64, 256),
        (4, 64, 256), (2, 4, 64, 128), (2, 4, 64, 128), (4, 2, 4, 128), (4, 2, 4, 128),
        (2, 2, 2, 2, 2, 128), (2, 2, 2, 2, 2, 128), (4, 4, 32, 128), (2, 4, 2, 32, 128), (2, 4, 2, 32, 128),
        (2, 32, 128), (1, 2, 32, 128), (1, 4, 32, 128), (4, 1, 2, 128), (4, 1, 2, 128),
        (2, 2, 2, 2, 128), (2, 2, 2, 2, 128), (2, 2, 2, 128), (2, 2, 16, 128),
        (2, 2, 2, 16, 128), (2, 2, 2, 16, 128), (2, 2, 16, 128),
    ]
    dma = pltpu.SemaphoreType.DMA
    hbm = pl.BlockSpec(memory_space=pl.ANY)
    vmem = pl.BlockSpec(memory_space=pltpu.VMEM)
    results = pl.pallas_call(
        functools.partial(kernel, nz, nx),
        out_shape=tuple(pltpu.VMEM(s, f32) for s in shapes),
        in_specs=[hbm] * 3,
        out_specs=(vmem,) * 4,
        scratch_shapes=[pltpu.VMEM(s, f32) if s else pltpu.VMEM((256, 256), jnp.bfloat16) for s in scratch]
        + [dma((6,)), dma((3, 2)), dma((3, 2)), dma((3, 2, 2)), dma((3, 2, 2)), dma((7, 2)), dma((7, 2)), dma((12, 2)), dma((12, 2))],
        compiler_params=pltpu.CompilerParams(collective_id=0, has_side_effects=True),
        name="wavelet",
    )(velocity, jnp.asarray(deinterleave(256), jnp.bfloat16), jnp.asarray(band_matrix(128)))
    return pl.pallas_call(
        place,
        out_shape=tuple(jax.ShapeDtypeStruct(s, f32) for s in shapes),
        in_specs=[vmem] * 4,
        out_specs=(hbm,) * 4,
        scratch_shapes=[dma((10,))],
        name="place",
    )(*(pltpu.with_memory_space_constraint(r, pltpu.VMEM) for r in results))


def solution(mesh):
    return jax.shard_map(
        functools.partial(on_device, mesh.shape["gz"], mesh.shape["gx"]),
        mesh=mesh,
        in_specs=(P("gz", "gx", None),),
        out_specs=(
            P(None, "gz", "gx", None),
            P(None, "gz", "gx", None),
            P(None, "gz", "gx", None),
            P("gz", "gx", None),
        ),
        check_vma=False,
    )
```

```python
import functools

import jax
import jax.numpy as jnp
import numpy as np
from jax import lax
from jax.experimental import pallas as pl
from jax.experimental.pallas import tpu as pltpu
from jax.sharding import PartitionSpec as P

LOW_TAPS = (
    0.026748757411,
    -0.016864118443,
    -0.078223266529,
    0.266864118443,
    0.602949018236,
    0.266864118443,
    -0.078223266529,
    -0.016864118443,
    0.026748757411,
)
HIGH_TAPS = (
    0.091271763114,
    -0.057543526229,
    -0.591271763114,
    1.115087052457,
    -0.591271763114,
    -0.057543526229,
    0.091271763114,
)

AL = -1.586134342059924
BE = -0.052980118572961
GA = 0.882911075530934
DE = 0.443506852043971
KL = 1.0 / 1.230174104914001
KH = 1.230174104914001
SCALE = (KL, KH)

UNITS = (2, 3, 2, 3, 2)

OWN_FIRST = 2

MESH = pl.DeviceIdType.MESH
HIGHEST = lax.Precision.HIGHEST


def band_matrix(n):
    half = n // 2
    w = np.zeros((n, n), np.float64)
    for j in range(half):
        for k in range(9):
            w[(2 * j + k - 4) % n, j] += LOW_TAPS[k]
        for k in range(7):
            w[(2 * j + 1 + k - 3) % n, half + j] += HIGH_TAPS[k]
    return w.astype(np.float32)


def edge_terms(get, n):
    a = get(n - 1) + AL * get(n - 2)
    b = get(n - 2) + BE * (get(n - 3) + AL * (get(n - 4) + get(n - 2)) + a)
    e = get(0)
    c = e + BE * (get(1) + AL * (e + get(2)))
    return a, b, e, c


def lift_planes(f, a, b, e_up, c):
    even, odd = f[0::2], f[1::2]
    n = len(even)
    even_next = even[1:] + [e_up]
    d1 = [odd[j] + AL * (even[j] + even_next[j]) for j in range(n)]
    d1m = a + AL * even[0]
    d1_prev = [d1m] + d1[:-1]
    s1 = [even[j] + BE * (d1_prev[j] + d1[j]) for j in range(n)]
    s1m = b + (AL * BE) * even[0]
    s1n = c + BE * d1[-1]
    s1_next = s1[1:] + [s1n]
    d2 = [d1[j] + GA * (s1[j] + s1_next[j]) for j in range(n)]
    d2m = d1m + GA * (s1m + s1[0])
    d2_prev = [d2m] + d2[:-1]
    s2 = [s1[j] + DE * (d2_prev[j] + d2[j]) for j in range(n)]
    return s2, d2


def from_above(x, row):
    n = x.shape[0]
    at = lax.broadcasted_iota(jnp.int32, x.shape, 0)
    return jnp.where(at == n - 1, row, pltpu.roll(x, n - 1, 0))


def from_below(x, row):
    at = lax.broadcasted_iota(jnp.int32, x.shape, 0)
    return jnp.where(at == 0, row, pltpu.roll(x, 1, 0))


def lift_rows(even, odd, a, b, e_up, c):
    n = even.shape[0]
    d1 = odd + AL * (even + from_above(even, e_up))
    d1m = a + AL * even[0:1]
    s1 = even + BE * (from_below(d1, d1m) + d1)
    s1m = b + (AL * BE) * even[0:1]
    s1n = c + BE * d1[n - 1 : n]
    d2 = d1 + GA * (s1 + from_above(s1, s1n))
    d2m = d1m + GA * (s1m + s1[0:1])
    s2 = s1 + DE * (from_below(d2, d2m) + d2)
    return s2, d2


def deinterleave(n):
    p = np.zeros((n, n), np.float32)
    for j in range(n // 2):
        p[2 * j, j] = p[2 * j + 1, n // 2 + j] = 1.0
    return p


def lift_lanes(x, pick):
    even, odd = [], []
    for b in range(x.shape[1] // 256):
        block = x[:, 256 * b : 256 * b + 256]
        parts = []
        for _ in range(3):
            parts.append(block.astype(jnp.bfloat16))
            block = block - parts[-1].astype(jnp.float32)
        out = sum(jnp.dot(part, pick, preferred_element_type=jnp.float32) for part in parts)
        even.append(out[:, :128])
        odd.append(out[:, 128:])
    n = len(even)
    lane = lax.broadcasted_iota(jnp.int32, even[0].shape, 1)

    def following(v):
        moved = [pltpu.roll(u, 127, 1) for u in v]
        return moved if n == 1 else [jnp.where(lane == 127, moved[(i + 1) % n], moved[i]) for i in range(n)]

    def preceding(v):
        moved = [pltpu.roll(u, 1, 1) for u in v]
        return moved if n == 1 else [jnp.where(lane == 0, moved[(i - 1) % n], moved[i]) for i in range(n)]

    def step(v, factor, w, shifted):
        return [p + factor * (q + r) for p, q, r in zip(v, w, shifted(w))]

    d1 = step(odd, AL, even, following)
    s1 = step(even, BE, d1, preceding)
    d2 = step(d1, GA, s1, following)
    s2 = step(s1, DE, d2, preceding)
    return [KL * u for u in s2] + [KH * u for u in d2]


def halo_effect(a, b, e, c):
    first = (GA * BE) * a
    before = a + GA * (b + BE * a)
    q = AL * e
    last = q + GA * (c + (2 * BE) * q)
    last_but = (GA * BE) * q
    low = (BE * a + DE * (before + first), DE * first, DE * last_but, BE * q + DE * (last_but + last))
    return low, (first, last_but, last)


def dot(x, w):
    return jnp.dot(x, w, precision=HIGHEST, preferred_element_type=jnp.float32)


def kernel(
    nz, nx,
    v_hbm, pick_hbm, w2_hbm, w3_hbm,
    one, two, three, coarse,
    f1, pick, w2, w3, y1, yz1, xz1, xs1, xr1, own1, zs1, zr1,
    f2, y2, xs2, xr2, own2, zs2, zr2,
    f3, y3, xs3, xr3, own3, zs3, zr3, zr3b,
    in_sem, xsend, xrecv, zsend, zrecv, usend, urecv,
):
    iz, ix = lax.axis_index("gz"), lax.axis_index("gx")
    right, left = lax.rem(ix + 1, nx), lax.rem(ix + nx - 1, nx)
    up, down = lax.rem(iz + 1, nz), lax.rem(iz + nz - 1, nz)
    up2, down2 = lax.rem(iz + 2, nz), lax.rem(iz + nz - 2, nz)

    near = lax.rem(iz, 2)
    sides = [(d, {"gz": lax.rem(iz + nz + 1 - 2 * d, nz)}) for d in (1 - near, near)]

    barrier = pltpu.get_barrier_semaphore()
    for k in (right, left):
        pl.semaphore_signal(barrier, inc=1, device_id={"gx": k}, device_id_type=MESH)
    for k in (up, down):
        pl.semaphore_signal(barrier, inc=1, device_id={"gz": k}, device_id_type=MESH)

    parts = (0, 3, 1, 2)
    loads = [
        pltpu.make_async_copy(v_hbm.at[:, pl.ds(32 * k, 32)], f1.at[:, pl.ds(32 * k, 32)], in_sem.at[i])
        for i, k in enumerate(parts)
    ]
    loads += [
        pltpu.make_async_copy(src, dst, in_sem.at[i]) for i, src, dst in ((4, pick_hbm, pick), (5, w3_hbm, w3), (6, w2_hbm, w2))
    ]
    for load in loads:
        load.start()

    sent = []

    def send(src, dst, send_sem, recv_sem, device):
        copy = pltpu.make_async_remote_copy(
            src_ref=src, dst_ref=dst, send_sem=send_sem, recv_sem=recv_sem,
            device_id=device, device_id_type=MESH,
        )
        copy.start()
        sent.append(copy)
        return copy

    def send_x(level, xs, xr):
        return [
            send(xs.at[0:2], xr.at[0:2], xsend.at[level, 0], xrecv.at[level, 0], {"gx": right}),
            send(xs.at[2:4], xr.at[2:4], xsend.at[level, 1], xrecv.at[level, 1], {"gx": left}),
        ]

    def send_z(slot, zs, zr, *at, which=(0, 1)):
        return [
            send(zs.at[(d,) + at], zr.at[(d,) + at], zsend.at[slot, d], zrecv.at[slot, d], device)
            for d, device in (sides[w] for w in which)
        ]

    units = [(g, k, r) for g in (1, 2, 3) for k in range(2) for r in range(2)]
    pending = list(units)
    on_way = {1: [], 2: [], 3: []}

    def send_units(count, which=(0, 1)):
        done = len(units) - len(pending)
        for i in range(done, done + count):
            g, k, r = units[i]
            at = pl.ds(32 * r, 32)
            for d, device in (sides[w] for w in which):
                on_way[g].append(
                    send(zs1.at[d, g, k, at], zr1.at[d, g, k, at], usend.at[i, d], urecv.at[i, d], device)
                )
        if which[-1] == 1:
            del pending[:count]

    def arrive(copies):
        for copy in copies:
            copy.wait_recv()

    def x_split(y, xr, put, some=None):
        chunks, planes, half = y.shape[0], y.shape[1], y.shape[2] // 2

        def plane(p):
            for c in range(chunks):
                even = y[c, p, pl.ds(0, half, stride=2), :]
                odd = y[c, p, pl.ds(1, half, stride=2), :]
                if xr is None:
                    terms = [jnp.zeros((1, 128), jnp.float32)] * 4
                else:
                    terms = [xr[k, c, pl.ds(p, 1), :] for k in range(4)]
                low, high = lift_rows(even, odd, *terms)
                put(c, 0, p, low)
                put(c, 1, p, high)

        if planes == 8:
            lax.fori_loop(0, planes // 2, lambda i, _: (plane(2 * i), plane(2 * i + 1), 0)[2], 0)
        else:
            for p in range(planes) if some is None else some:
                plane(p)

    def into(own, wide):
        def put(c, xb, p, value):
            own[2 * (c // wide) + xb, p, :, pl.ds(128 * (c % wide), 128)] = value

        return put

    def z_terms(own, zs, groups, step):
        planes, rows = own.shape[1], own.shape[2]
        for g in groups:
            def chunk(i, _):
                at = pl.ds(pl.multiple_of(i * step, step), step)
                terms = edge_terms(lambda k: own[g, k, at, :], planes)
                for k in range(4):
                    zs[k // 2, g, k % 2, at, :] = terms[k]
                return 0

            lax.fori_loop(0, rows // step, chunk, 0)

    def z_split(own, zr, g, step, low_to, high_to):
        planes, rows = own.shape[1], own.shape[2]

        def chunk(i, _):
            at = pl.ds(pl.multiple_of(i * step, step), step)
            f = [own[g, k, at, :] for k in range(planes)]
            terms = [zr[k // 2, g, k % 2, at, :] for k in range(4)]
            low, high = lift_planes(f, *terms)
            for j in range(planes // 2):
                low_to[j, at, :] = low[j] * (KL * SCALE[g % 2])
                high_to[j, at, :] = high[j] * (KH * SCALE[g % 2])
            return 0

        lax.fori_loop(0, rows // step, chunk, 0)

    def bands(out, g):
        return out.at[2 * g - 1], out.at[2 * g]

    for i, part in enumerate(parts):
        loads[i].wait()
        at = pl.ds(32 * part, 32)
        for c in range(4):
            terms = edge_terms(lambda k: f1[k, at, pl.ds(128 * c, 128)], f1.shape[0])
            for k in range(4):
                yz1[c, k, at, :] = terms[k]

    def put_raw(c, xb, p, value):
        xz1[xb, p, :, pl.ds(128 * c, 128)] = value

    def terms_of(xb, planes, extra=()):
        rows = [xz1[xb, p] for p in planes]
        out = lift_lanes(jnp.concatenate([*rows, *extra], 0), pick[...])
        for c in range(4):
            for i, p in enumerate(planes):
                zs1[p // 2, 2 * (c // 2) + xb, lax.rem(p, 2), :, pl.ds(128 * (c % 2), 128)] = out[c][64 * i : 64 * i + 64]
        return [out_c[64 * len(planes) :] for out_c in out]

    pairs = [[2 * d, 2 * d + 1] for d, _ in sides]
    x_split(yz1, None, put_raw, pairs[0])
    edges = edge_terms(lambda k: f1[:, k, :], f1.shape[1])
    loads[4].wait()
    out = terms_of(0, pairs[0], edges)
    for k in range(4):
        for c in range(4):
            xs1[k, c] = out[c][8 * k : 8 * k + 8]
    pl.semaphore_wait(barrier, 4)
    x1 = send_x(0, xs1, xr1)
    inner = (0, slice(None), pl.ds(8, 48))
    z1 = send_z(0, zs1, zr1, *inner, which=(0,))
    x_split(yz1, None, put_raw, pairs[1])
    terms_of(0, pairs[1])
    z1 += send_z(0, zs1, zr1, *inner, which=(1,))
    terms_of(1, range(4))

    def rows(i, _):
        at = pl.ds(2 * i, 2)
        out = lift_lanes(f1[at].reshape(256, 512), pick[...])
        for c in range(4):
            y1[c, at] = out[c].reshape(2, 128, 128)
        return 0

    lax.fori_loop(0, OWN_FIRST, rows, 0)
    arrive(x1)
    for c in range(4):
        g, lanes = 2 * (c // 2), pl.ds(128 * (c % 2), 128)
        terms = [edge_terms(lambda i: xr1[k, c, i : i + 1, :], 8) for k in range(4)]
        for p in range(4):
            low, high = halo_effect(*(terms[k][p] for k in range(4)))
            for r, effect in zip((0, 1, 62, 63), low):
                zs1[p // 2, g, p % 2, r : r + 1, lanes] += effect
            for r, effect in zip((0, 62, 63), high):
                zs1[p // 2, g + 1, p % 2, r : r + 1, lanes] += effect
    z1 += send_z(1, zs1, zr1, 0, slice(None), pl.ds(0, 8)) + send_z(2, zs1, zr1, 0, slice(None), pl.ds(56, 8))
    send_units(UNITS[0])
    lax.fori_loop(OWN_FIRST, f1.shape[0] // 2, rows, 0)
    x_split(y1, xr1, into(own1, 2))

    arrive(z1)
    z_split(own1, zr1, 0, 8, f2, one.at[0])

    loads[6].wait()
    edges = edge_terms(lambda k: f2[:, k, :], f2.shape[1])
    out = dot(jnp.concatenate(edges, 0), w2[...])
    for k in range(4):
        for c in range(2):
            xs2[k, c] = out[4 * k : 4 * k + 4, 128 * c : 128 * c + 128]
    x2 = send_x(1, xs2, xr2)
    send_units(UNITS[1])
    out = dot(f2[...].reshape(256, 256), w2[...])
    for c in range(2):
        y2[c] = out[:, 128 * c : 128 * c + 128].reshape(4, 64, 128)
    arrive(x2)
    x_split(y2, xr2, into(own2, 1))
    z_terms(own2, zs2, range(4), 32)
    z2 = send_z(3, zs2, zr2, 0)
    send_units(UNITS[2])
    arrive(z2)
    z_split(own2, zr2, 0, 32, f3, two.at[0])

    loads[5].wait()
    y3[0] = dot(f3[...].reshape(64, 128), w3[...]).reshape(2, 32, 128)
    for k, term in enumerate(edge_terms(lambda k: y3[0, :, k, :], 32)):
        xs3[k, 0] = term
    x3 = send_x(2, xs3, xr3)
    send_units(UNITS[3])
    arrive(x3)
    x_split(y3, xr3, into(own3, 1))
    for xb in range(2):
        even, odd = own3[xb, 0], own3[xb, 1]
        a = odd + AL * even
        zs3[0, 0, xb] = a
        zs3[0, 1, xb] = even + BE * (AL * even + a)
        zs3[1, 0, xb] = even
        zs3[1, 1, xb] = even + BE * a
    z3 = send_z(5, zs3, zr3) + [
        send(zs3.at[d, 0], zr3b.at[d], zsend.at[6, d], zrecv.at[6, d], {"gz": k})
        for d, k in ((0, up2), (1, down2))
    ]
    z2 = []
    for w in range(2):
        send_units(UNITS[4], (w,))
        z2 += send_z(4, zs2, zr2, pl.ds(1, 3), which=(w,))
    for g in (1, 2):
        arrive(on_way[g])
        z_split(own1, zr1, g, 8, *bands(one, g))
    arrive(z3)
    for xb in range(2):
        a, b, e, c = (zr3[k // 2, k % 2, xb] for k in range(4))
        b = b + BE * zr3b[0, xb]
        c = c + (AL * BE) * zr3b[1, xb]
        low, high = lift_planes([own3[xb, 0], own3[xb, 1]], a, b, e, c)
        low, high = low[0] * (KL * SCALE[xb]), high[0] * (KH * SCALE[xb])
        for yb in range(2):
            lanes = slice(64 * yb, 64 * yb + 64)
            band = 2 * xb + 4 * yb
            if band == 0:
                coarse[0] = low[:, lanes]
            else:
                three[band - 1, 0] = low[:, lanes]
            three[band, 0] = high[:, lanes]
    arrive(on_way[3])
    z_split(own1, zr1, 3, 8, *bands(one, 3))
    arrive(z2)
    for g in (1, 2, 3):
        z_split(own2, zr2, g, 32, *bands(two, g))
    for copy in sent:
        copy.wait_send()


def place(one, two, three, coarse, one_to, two_to, three_to, coarse_to, sem):
    pairs = [(one.at[b], one_to.at[b]) for b in range(7)]
    pairs += [(two, two_to), (three, three_to), (coarse, coarse_to)]
    copies = [pltpu.make_async_copy(src, dst, sem.at[i]) for i, (src, dst) in enumerate(pairs)]
    for copy in copies:
        copy.start()
    for copy in copies:
        copy.wait()


def on_device(nz, nx, velocity):
    f32 = jnp.float32
    shapes = [(7, 4, 64, 256), (7, 2, 32, 128), (7, 1, 16, 64), (1, 16, 64)]
    scratch = [
        (8, 128, 512), None, (256, 256), (128, 128),
        (4, 8, 128, 128), (4, 4, 128, 128), (2, 4, 64, 512), (4, 4, 8, 128), (4, 4, 8, 128), (4, 8, 64, 256), (2, 4, 2, 64, 256), (2, 4, 2, 64, 256),
        (4, 64, 256), (2, 4, 64, 128), (4, 2, 4, 128), (4, 2, 4, 128), (4, 4, 32, 128), (2, 4, 2, 32, 128), (2, 4, 2, 32, 128),
        (2, 32, 128), (1, 2, 32, 128), (4, 1, 2, 128), (4, 1, 2, 128), (2, 2, 16, 128), (2, 2, 2, 16, 128), (2, 2, 2, 16, 128), (2, 2, 16, 128),
    ]
    dma = pltpu.SemaphoreType.DMA
    hbm = pl.BlockSpec(memory_space=pl.ANY)
    vmem = pl.BlockSpec(memory_space=pltpu.VMEM)
    results = pl.pallas_call(
        functools.partial(kernel, nz, nx),
        out_shape=tuple(pltpu.VMEM(s, f32) for s in shapes),
        in_specs=[hbm] * 4,
        out_specs=(vmem,) * 4,
        scratch_shapes=[pltpu.VMEM(s, f32) if s else pltpu.VMEM((256, 256), jnp.bfloat16) for s in scratch]
        + [dma((7,)), dma((3, 2)), dma((3, 2)), dma((7, 2)), dma((7, 2)), dma((12, 2)), dma((12, 2))],
        compiler_params=pltpu.CompilerParams(collective_id=0, has_side_effects=True),
        name="wavelet",
    )(velocity, jnp.asarray(deinterleave(256), jnp.bfloat16), jnp.asarray(band_matrix(256)), jnp.asarray(band_matrix(128)))
    return pl.pallas_call(
        place,
        out_shape=tuple(jax.ShapeDtypeStruct(s, f32) for s in shapes),
        in_specs=[vmem] * 4,
        out_specs=(hbm,) * 4,
        scratch_shapes=[dma((10,))],
        name="place",
    )(*(pltpu.with_memory_space_constraint(r, pltpu.VMEM) for r in results))


def solution(mesh):
    return jax.shard_map(
        functools.partial(on_device, mesh.shape["gz"], mesh.shape["gx"]),
        mesh=mesh,
        in_specs=(P("gz", "gx", None),),
        out_specs=(
            P(None, "gz", "gx", None),
            P(None, "gz", "gx", None),
            P(None, "gz", "gx", None),
            P("gz", "gx", None),
        ),
        check_vma=False,
    )
```

```python
import functools

import jax
import jax.numpy as jnp
import numpy as np
from jax import lax
from jax.experimental import pallas as pl
from jax.experimental.pallas import tpu as pltpu
from jax.sharding import PartitionSpec as P

LOW_TAPS = (
    0.026748757411,
    -0.016864118443,
    -0.078223266529,
    0.266864118443,
    0.602949018236,
    0.266864118443,
    -0.078223266529,
    -0.016864118443,
    0.026748757411,
)
HIGH_TAPS = (
    0.091271763114,
    -0.057543526229,
    -0.591271763114,
    1.115087052457,
    -0.591271763114,
    -0.057543526229,
    0.091271763114,
)

AL = -1.586134342059924
BE = -0.052980118572961
GA = 0.882911075530934
DE = 0.443506852043971
KL = 1.0 / 1.230174104914001
KH = 1.230174104914001
SCALE = (KL, KH)

UNITS = (2, 3, 2, 4, 1)

OWN_FIRST = 2

MESH = pl.DeviceIdType.MESH
HIGHEST = lax.Precision.HIGHEST


def band_matrix(n):
    half = n // 2
    w = np.zeros((n, n), np.float64)
    for j in range(half):
        for k in range(9):
            w[(2 * j + k - 4) % n, j] += LOW_TAPS[k]
        for k in range(7):
            w[(2 * j + 1 + k - 3) % n, half + j] += HIGH_TAPS[k]
    return w.astype(np.float32)


def edge_terms(get, n):
    a = get(n - 1) + AL * get(n - 2)
    b = get(n - 2) + BE * (get(n - 3) + AL * (get(n - 4) + get(n - 2)) + a)
    e = get(0)
    c = e + BE * (get(1) + AL * (e + get(2)))
    return a, b, e, c


def lift_planes(f, a, b, e_up, c):
    even, odd = f[0::2], f[1::2]
    n = len(even)
    even_next = even[1:] + [e_up]
    d1 = [odd[j] + AL * (even[j] + even_next[j]) for j in range(n)]
    d1m = a + AL * even[0]
    d1_prev = [d1m] + d1[:-1]
    s1 = [even[j] + BE * (d1_prev[j] + d1[j]) for j in range(n)]
    s1m = b + (AL * BE) * even[0]
    s1n = c + BE * d1[-1]
    s1_next = s1[1:] + [s1n]
    d2 = [d1[j] + GA * (s1[j] + s1_next[j]) for j in range(n)]
    d2m = d1m + GA * (s1m + s1[0])
    d2_prev = [d2m] + d2[:-1]
    s2 = [s1[j] + DE * (d2_prev[j] + d2[j]) for j in range(n)]
    return s2, d2


def from_above(x, row):
    n = x.shape[0]
    at = lax.broadcasted_iota(jnp.int32, x.shape, 0)
    return jnp.where(at == n - 1, row, pltpu.roll(x, n - 1, 0))


def from_below(x, row):
    at = lax.broadcasted_iota(jnp.int32, x.shape, 0)
    return jnp.where(at == 0, row, pltpu.roll(x, 1, 0))


def lift_rows(even, odd, a, b, e_up, c):
    n = even.shape[0]
    d1 = odd + AL * (even + from_above(even, e_up))
    d1m = a + AL * even[0:1]
    s1 = even + BE * (from_below(d1, d1m) + d1)
    s1m = b + (AL * BE) * even[0:1]
    s1n = c + BE * d1[n - 1 : n]
    d2 = d1 + GA * (s1 + from_above(s1, s1n))
    d2m = d1m + GA * (s1m + s1[0:1])
    s2 = s1 + DE * (from_below(d2, d2m) + d2)
    return s2, d2


def deinterleave(n):
    p = np.zeros((n, n), np.float32)
    for j in range(n // 2):
        p[2 * j, j] = p[2 * j + 1, n // 2 + j] = 1.0
    return p


def lift_lanes(x, pick):
    even, odd = [], []
    for b in range(x.shape[1] // 256):
        block = x[:, 256 * b : 256 * b + 256]
        parts = []
        for _ in range(3):
            parts.append(block.astype(jnp.bfloat16))
            block = block - parts[-1].astype(jnp.float32)
        out = sum(jnp.dot(part, pick, preferred_element_type=jnp.float32) for part in parts)
        even.append(out[:, :128])
        odd.append(out[:, 128:])
    n = len(even)
    lane = lax.broadcasted_iota(jnp.int32, even[0].shape, 1)

    def following(v):
        moved = [pltpu.roll(u, 127, 1) for u in v]
        return moved if n == 1 else [jnp.where(lane == 127, moved[(i + 1) % n], moved[i]) for i in range(n)]

    def preceding(v):
        moved = [pltpu.roll(u, 1, 1) for u in v]
        return moved if n == 1 else [jnp.where(lane == 0, moved[(i - 1) % n], moved[i]) for i in range(n)]

    def step(v, factor, w, shifted):
        return [p + factor * (q + r) for p, q, r in zip(v, w, shifted(w))]

    d1 = step(odd, AL, even, following)
    s1 = step(even, BE, d1, preceding)
    d2 = step(d1, GA, s1, following)
    s2 = step(s1, DE, d2, preceding)
    return [KL * u for u in s2] + [KH * u for u in d2]


def halo_effect(a, b, e, c):
    first = (GA * BE) * a
    before = a + GA * (b + BE * a)
    q = AL * e
    last = q + GA * (c + (2 * BE) * q)
    last_but = (GA * BE) * q
    low = (BE * a + DE * (before + first), DE * first, DE * last_but, BE * q + DE * (last_but + last))
    return low, (first, last_but, last)


def dot(x, w):
    return jnp.dot(x, w, precision=HIGHEST, preferred_element_type=jnp.float32)


def kernel(
    nz, nx,
    v_hbm, pick_hbm, w2_hbm, w3_hbm,
    one, two, three, coarse,
    f1, pick, w2, w3, y1, yz1, xz1, xs1, xr1, own1, zs1, zr1,
    f2, y2, xs2, xr2, own2, zs2, zr2,
    f3, y3, xs3, xr3, own3, zs3, zr3, zr3b,
    in_sem, xsend, xrecv, zsend, zrecv, usend, urecv,
):
    iz, ix = lax.axis_index("gz"), lax.axis_index("gx")
    right, left = lax.rem(ix + 1, nx), lax.rem(ix + nx - 1, nx)
    up, down = lax.rem(iz + 1, nz), lax.rem(iz + nz - 1, nz)
    up2, down2 = lax.rem(iz + 2, nz), lax.rem(iz + nz - 2, nz)

    near = lax.rem(iz, 2)
    sides = [(d, {"gz": lax.rem(iz + nz + 1 - 2 * d, nz)}) for d in (1 - near, near)]

    barrier = pltpu.get_barrier_semaphore()
    for k in (right, left):
        pl.semaphore_signal(barrier, inc=1, device_id={"gx": k}, device_id_type=MESH)
    for k in (up, down):
        pl.semaphore_signal(barrier, inc=1, device_id={"gz": k}, device_id_type=MESH)

    parts = (0, 3, 1, 2)
    loads = [
        pltpu.make_async_copy(v_hbm.at[:, pl.ds(32 * k, 32)], f1.at[:, pl.ds(32 * k, 32)], in_sem.at[i])
        for i, k in enumerate(parts)
    ]
    loads += [
        pltpu.make_async_copy(src, dst, in_sem.at[i]) for i, src, dst in ((4, pick_hbm, pick), (5, w3_hbm, w3), (6, w2_hbm, w2))
    ]
    for load in loads:
        load.start()

    sent = []

    def send(src, dst, send_sem, recv_sem, device):
        copy = pltpu.make_async_remote_copy(
            src_ref=src, dst_ref=dst, send_sem=send_sem, recv_sem=recv_sem,
            device_id=device, device_id_type=MESH,
        )
        copy.start()
        sent.append(copy)
        return copy

    def send_x(level, xs, xr):
        return [
            send(xs.at[0:2], xr.at[0:2], xsend.at[level, 0], xrecv.at[level, 0], {"gx": right}),
            send(xs.at[2:4], xr.at[2:4], xsend.at[level, 1], xrecv.at[level, 1], {"gx": left}),
        ]

    def send_z(slot, zs, zr, *at, which=(0, 1)):
        return [
            send(zs.at[(d,) + at], zr.at[(d,) + at], zsend.at[slot, d], zrecv.at[slot, d], device)
            for d, device in (sides[w] for w in which)
        ]

    units = [(g, k, r) for g in (1, 2, 3) for k in range(2) for r in range(2)]
    pending = list(units)
    on_way = {1: [], 2: [], 3: []}

    def send_units(count, which=(0, 1)):
        done = len(units) - len(pending)
        for i in range(done, done + count):
            g, k, r = units[i]
            at = pl.ds(32 * r, 32)
            for d, device in (sides[w] for w in which):
                on_way[g].append(
                    send(zs1.at[d, g, k, at], zr1.at[d, g, k, at], usend.at[i, d], urecv.at[i, d], device)
                )
        if which[-1] == 1:
            del pending[:count]

    def arrive(copies):
        for copy in copies:
            copy.wait_recv()

    def x_split(y, xr, put, some=None):
        chunks, planes, half = y.shape[0], y.shape[1], y.shape[2] // 2

        def plane(p):
            for c in range(chunks):
                even = y[c, p, pl.ds(0, half, stride=2), :]
                odd = y[c, p, pl.ds(1, half, stride=2), :]
                if xr is None:
                    terms = [jnp.zeros((1, 128), jnp.float32)] * 4
                else:
                    terms = [xr[k, c, pl.ds(p, 1), :] for k in range(4)]
                low, high = lift_rows(even, odd, *terms)
                put(c, 0, p, low)
                put(c, 1, p, high)

        if planes == 8:
            lax.fori_loop(0, planes // 2, lambda i, _: (plane(2 * i), plane(2 * i + 1), 0)[2], 0)
        else:
            for p in range(planes) if some is None else some:
                plane(p)

    def into(own, wide):
        def put(c, xb, p, value):
            own[2 * (c // wide) + xb, p, :, pl.ds(128 * (c % wide), 128)] = value

        return put

    def z_terms(own, zs, groups, step):
        planes, rows = own.shape[1], own.shape[2]
        for g in groups:
            def chunk(i, _):
                at = pl.ds(pl.multiple_of(i * step, step), step)
                terms = edge_terms(lambda k: own[g, k, at, :], planes)
                for k in range(4):
                    zs[k // 2, g, k % 2, at, :] = terms[k]
                return 0

            lax.fori_loop(0, rows // step, chunk, 0)

    def z_split(own, zr, g, step, low_to, high_to):
        planes, rows = own.shape[1], own.shape[2]

        def chunk(i, _):
            at = pl.ds(pl.multiple_of(i * step, step), step)
            f = [own[g, k, at, :] for k in range(planes)]
            terms = [zr[k // 2, g, k % 2, at, :] for k in range(4)]
            low, high = lift_planes(f, *terms)
            for j in range(planes // 2):
                low_to[j, at, :] = low[j] * (KL * SCALE[g % 2])
                high_to[j, at, :] = high[j] * (KH * SCALE[g % 2])
            return 0

        lax.fori_loop(0, rows // step, chunk, 0)

    def bands(out, g):
        return out.at[2 * g - 1], out.at[2 * g]

    for i, part in enumerate(parts):
        loads[i].wait()
        at = pl.ds(32 * part, 32)
        for c in range(4):
            terms = edge_terms(lambda k: f1[k, at, pl.ds(128 * c, 128)], f1.shape[0])
            for k in range(4):
                yz1[c, k, at, :] = terms[k]

    def put_raw(c, xb, p, value):
        xz1[xb, p, :, pl.ds(128 * c, 128)] = value

    def terms_of(xb, planes, extra=()):
        rows = [xz1[xb, p] for p in planes]
        out = lift_lanes(jnp.concatenate([*rows, *extra], 0), pick[...])
        for c in range(4):
            for i, p in enumerate(planes):
                zs1[p // 2, 2 * (c // 2) + xb, lax.rem(p, 2), :, pl.ds(128 * (c % 2), 128)] = out[c][64 * i : 64 * i + 64]
        return [out_c[64 * len(planes) :] for out_c in out]

    pairs = [[2 * d, 2 * d + 1] for d, _ in sides]
    x_split(yz1, None, put_raw, pairs[0])
    edges = edge_terms(lambda k: f1[:, k, :], f1.shape[1])
    loads[4].wait()
    out = terms_of(0, pairs[0], edges)
    for k in range(4):
        for c in range(4):
            xs1[k, c] = out[c][8 * k : 8 * k + 8]
    pl.semaphore_wait(barrier, 4)
    x1 = send_x(0, xs1, xr1)
    inner = (0, slice(None), pl.ds(8, 48))
    z1 = send_z(0, zs1, zr1, *inner, which=(0,))
    x_split(yz1, None, put_raw, pairs[1])
    terms_of(0, pairs[1])
    z1 += send_z(0, zs1, zr1, *inner, which=(1,))
    terms_of(1, range(4))

    def rows(i, _):
        at = pl.ds(2 * i, 2)
        out = lift_lanes(f1[at].reshape(256, 512), pick[...])
        for c in range(4):
            y1[c, at] = out[c].reshape(2, 128, 128)
        return 0

    lax.fori_loop(0, OWN_FIRST, rows, 0)
    arrive(x1)
    for c in range(4):
        g, lanes = 2 * (c // 2), pl.ds(128 * (c % 2), 128)
        terms = [edge_terms(lambda i: xr1[k, c, i : i + 1, :], 8) for k in range(4)]
        for p in range(4):
            low, high = halo_effect(*(terms[k][p] for k in range(4)))
            for r, effect in zip((0, 1, 62, 63), low):
                zs1[p // 2, g, p % 2, r : r + 1, lanes] += effect
            for r, effect in zip((0, 62, 63), high):
                zs1[p // 2, g + 1, p % 2, r : r + 1, lanes] += effect
    z1 += send_z(1, zs1, zr1, 0, slice(None), pl.ds(0, 8)) + send_z(2, zs1, zr1, 0, slice(None), pl.ds(56, 8))
    for w in range(2):
        send_units(UNITS[0], (w,))
    lax.fori_loop(OWN_FIRST, f1.shape[0] // 2, rows, 0)
    x_split(y1, xr1, into(own1, 2))

    arrive(z1)
    z_split(own1, zr1, 0, 8, f2, one.at[0])

    loads[6].wait()
    edges = edge_terms(lambda k: f2[:, k, :], f2.shape[1])
    out = dot(jnp.concatenate(edges, 0), w2[...])
    for k in range(4):
        for c in range(2):
            xs2[k, c] = out[4 * k : 4 * k + 4, 128 * c : 128 * c + 128]
    x2 = send_x(1, xs2, xr2)
    for w in range(2):
        send_units(UNITS[1], (w,))
    out = dot(f2[...].reshape(256, 256), w2[...])
    for c in range(2):
        y2[c] = out[:, 128 * c : 128 * c + 128].reshape(4, 64, 128)
    arrive(x2)
    x_split(y2, xr2, into(own2, 1))
    z_terms(own2, zs2, range(4), 32)
    z2 = send_z(3, zs2, zr2, 0)
    for w in range(2):
        send_units(UNITS[2], (w,))
    arrive(z2)
    z_split(own2, zr2, 0, 32, f3, two.at[0])

    loads[5].wait()
    y3[0] = dot(f3[...].reshape(64, 128), w3[...]).reshape(2, 32, 128)
    for k, term in enumerate(edge_terms(lambda k: y3[0, :, k, :], 32)):
        xs3[k, 0] = term
    x3 = send_x(2, xs3, xr3)
    for w in range(2):
        send_units(UNITS[3], (w,))
    arrive(x3)
    x_split(y3, xr3, into(own3, 1))
    for xb in range(2):
        even, odd = own3[xb, 0], own3[xb, 1]
        a = odd + AL * even
        zs3[0, 0, xb] = a
        zs3[0, 1, xb] = even + BE * (AL * even + a)
        zs3[1, 0, xb] = even
        zs3[1, 1, xb] = even + BE * a
    z3 = send_z(5, zs3, zr3) + [
        send(zs3.at[d, 0], zr3b.at[d], zsend.at[6, d], zrecv.at[6, d], {"gz": k})
        for d, k in ((0, up2), (1, down2))
    ]
    z2 = []
    for w in range(2):
        send_units(UNITS[4], (w,))
        z2 += send_z(4, zs2, zr2, pl.ds(1, 3), which=(w,))
    for g in (1, 2):
        arrive(on_way[g])
        z_split(own1, zr1, g, 8, *bands(one, g))
    arrive(z3)
    for xb in range(2):
        a, b, e, c = (zr3[k // 2, k % 2, xb] for k in range(4))
        b = b + BE * zr3b[0, xb]
        c = c + (AL * BE) * zr3b[1, xb]
        low, high = lift_planes([own3[xb, 0], own3[xb, 1]], a, b, e, c)
        low, high = low[0] * (KL * SCALE[xb]), high[0] * (KH * SCALE[xb])
        for yb in range(2):
            lanes = slice(64 * yb, 64 * yb + 64)
            band = 2 * xb + 4 * yb
            if band == 0:
                coarse[0] = low[:, lanes]
            else:
                three[band - 1, 0] = low[:, lanes]
            three[band, 0] = high[:, lanes]
    arrive(on_way[3])
    z_split(own1, zr1, 3, 8, *bands(one, 3))
    arrive(z2)
    for g in (1, 2, 3):
        z_split(own2, zr2, g, 32, *bands(two, g))
    for copy in sent:
        copy.wait_send()


def place(one, two, three, coarse, one_to, two_to, three_to, coarse_to, sem):
    pairs = [(one.at[b], one_to.at[b]) for b in range(7)]
    pairs += [(two, two_to), (three, three_to), (coarse, coarse_to)]
    copies = [pltpu.make_async_copy(src, dst, sem.at[i]) for i, (src, dst) in enumerate(pairs)]
    for copy in copies:
        copy.start()
    for copy in copies:
        copy.wait()


def on_device(nz, nx, velocity):
    f32 = jnp.float32
    shapes = [(7, 4, 64, 256), (7, 2, 32, 128), (7, 1, 16, 64), (1, 16, 64)]
    scratch = [
        (8, 128, 512), None, (256, 256), (128, 128),
        (4, 8, 128, 128), (4, 4, 128, 128), (2, 4, 64, 512), (4, 4, 8, 128), (4, 4, 8, 128), (4, 8, 64, 256), (2, 4, 2, 64, 256), (2, 4, 2, 64, 256),
        (4, 64, 256), (2, 4, 64, 128), (4, 2, 4, 128), (4, 2, 4, 128), (4, 4, 32, 128), (2, 4, 2, 32, 128), (2, 4, 2, 32, 128),
        (2, 32, 128), (1, 2, 32, 128), (4, 1, 2, 128), (4, 1, 2, 128), (2, 2, 16, 128), (2, 2, 2, 16, 128), (2, 2, 2, 16, 128), (2, 2, 16, 128),
    ]
    dma = pltpu.SemaphoreType.DMA
    hbm = pl.BlockSpec(memory_space=pl.ANY)
    vmem = pl.BlockSpec(memory_space=pltpu.VMEM)
    results = pl.pallas_call(
        functools.partial(kernel, nz, nx),
        out_shape=tuple(pltpu.VMEM(s, f32) for s in shapes),
        in_specs=[hbm] * 4,
        out_specs=(vmem,) * 4,
        scratch_shapes=[pltpu.VMEM(s, f32) if s else pltpu.VMEM((256, 256), jnp.bfloat16) for s in scratch]
        + [dma((7,)), dma((3, 2)), dma((3, 2)), dma((7, 2)), dma((7, 2)), dma((12, 2)), dma((12, 2))],
        compiler_params=pltpu.CompilerParams(collective_id=0, has_side_effects=True),
        name="wavelet",
    )(velocity, jnp.asarray(deinterleave(256), jnp.bfloat16), jnp.asarray(band_matrix(256)), jnp.asarray(band_matrix(128)))
    return pl.pallas_call(
        place,
        out_shape=tuple(jax.ShapeDtypeStruct(s, f32) for s in shapes),
        in_specs=[vmem] * 4,
        out_specs=(hbm,) * 4,
        scratch_shapes=[dma((10,))],
        name="place",
    )(*(pltpu.with_memory_space_constraint(r, pltpu.VMEM) for r in results))


def solution(mesh):
    return jax.shard_map(
        functools.partial(on_device, mesh.shape["gz"], mesh.shape["gx"]),
        mesh=mesh,
        in_specs=(P("gz", "gx", None),),
        out_specs=(
            P(None, "gz", "gx", None),
            P(None, "gz", "gx", None),
            P(None, "gz", "gx", None),
            P("gz", "gx", None),
        ),
        check_vma=False,
    )
```
